256 devices in a mesh: aux: 32 (over y, x, core), orb: 8 (over z).
Axes of the slice: x: 4, y: 4, z: 8, core: 2. Of those that a mesh axis runs over, the one named last changes fastest.
Arguments:
- band_pattern: int32 [256, 8], P('aux'), may hold values 0 or 1
- density_in: bfloat16 [256, 8, 128, 128], P('aux', 'orb')
- field_terms: bfloat16 [2, 256, 8, 128, 128], P(None, 'aux', 'orb'), may hold values from -3 to 3
- fit_blocks: int32 [1], replicated, may hold values from 0 to 255
- tensor: bfloat16 [1, 3072, 8, 16384], P(None, 'aux', 'orb'), may hold values from -0.015625 to 0.015625
- metric_inv: float32 [1, 3072, 3072], P(None, 'aux')
Outputs:
- response: bfloat16 [2, 256, 8, 128, 128], P(None, 'aux', 'orb')
- coefficients: float32 [1, 2, 3072], P(None, None, 'aux')
The draws below stay inside these ranges and needn't reach their ends.
All inputs are finite; a program needn't handle non-finite values. No bound on the sum of `band_pattern` on one device may be relied on, other than what follows from the above.
Results may differ from the reference program's by a relative error of at most 0.0055.
Values may be sent and summed in bfloat16 or wider, within the bound.
A program may use at most 192 MiB of HBM per device.

```python
import math
import jax
import jax.numpy as jnp
from jax import lax

BLK = 128
FIELDS = 2
NFIT = 1
NAUX = 3072
SLOTS = 8
NBLK = 256


def draw_density_in(key, part):
    full_shape = (NBLK, SLOTS, BLK, BLK)
    spread = 0.6 / math.sqrt(SLOTS * BLK)
    random_part = jax.random.normal(key, full_shape, jnp.float32) * spread
    slot_flag = (jnp.arange(SLOTS) == SLOTS // 2).astype(jnp.float32)[None, :, None, None]
    diagonal = slot_flag * jnp.eye(BLK, dtype=jnp.float32)[None, None] * 0.5
    return (random_part + diagonal).astype(jnp.bfloat16)


def draw_metric_inv(key, part):
    full_shape = (NFIT, NAUX, NAUX)
    spread = 0.5 / math.sqrt(NAUX)
    random_part = jax.random.normal(key, full_shape, jnp.float32) * spread
    return random_part + jnp.eye(NAUX, dtype=jnp.float32)[None]


def plant(result, stream_key, low, high):
    longest = result.shape.index(max(result.shape))
    spots = []
    for shift in (0, 1):
        where = [jax.random.randint(jax.random.fold_in(stream_key, axis), (), 0, length) for axis, length in enumerate(result.shape)]
        where[longest] = (where[longest] + shift) % result.shape[longest]
        spots.append(tuple(where))
    return result.at[spots[0]].set(low).at[spots[1]].set(high)


def steps_of(key, extent, cuts, smallest, top_value):
    factor_of = 1.0
    for dim, shards_of in cuts:
        heights = jax.random.uniform(jax.random.fold_in(jax.random.fold_in(key, 6), dim), (shards_of,), jnp.float32, smallest / len(cuts), top_value / len(cuts))
        factor_of = factor_of * jnp.repeat(jnp.exp(heights), extent[dim] // shards_of).reshape((-1,) + (1,) * (len(extent) - 1 - dim))
    return factor_of


def bell_draw(rng, shape, width, bound, cuts=(), held_as=jnp.bfloat16):
    entries = jax.random.normal(rng, shape, jnp.float32) * width
    if len(cuts) > 0:
        entries = steps_of(rng, shape, cuts, -0.22, 0.18) * entries
    return jnp.clip(entries, min=-bound, max=bound).astype(held_as)


def setup_inputs(seed: int = 0) -> dict:
    arg_keys = jax.random.split(jax.random.key(seed), 7)
    band_pattern = plant((jax.random.randint(arg_keys[0], (NBLK, SLOTS), 0, 4) < 3).astype(jnp.int32), jax.random.fold_in(arg_keys[0], 1), 0, 1)
    density_in = draw_density_in(jax.random.fold_in(arg_keys[6], 71), 0)
    field_terms = bell_draw(arg_keys[2], (FIELDS, NBLK, SLOTS, BLK, BLK), 0.5, 3.0, ((1, 32), (2, 8)))
    fit_blocks = jax.random.randint(arg_keys[3], (NFIT,), 0, NBLK).astype(jnp.int32)
    tensor = bell_draw(arg_keys[4], (NFIT, NAUX, SLOTS, BLK * BLK), (SLOTS * BLK * BLK) ** -0.5, 0.015625, ((1, 32), (2, 8)))
    metric_inv = draw_metric_inv(jax.random.fold_in(arg_keys[6], 71), 0)
    return {"band_pattern": band_pattern, "density_in": density_in, "field_terms": field_terms, "fit_blocks": fit_blocks, "tensor": tensor, "metric_inv": metric_inv}


def slide_slots(blocks, offset):
    slot_count = blocks.shape[2]
    if offset >= 0:
        padded = jnp.pad(blocks, ((0, 0), (0, 0), (offset, 0), (0, 0), (0, 0)))
        return padded[:, :, :slot_count]
    padded = jnp.pad(blocks, ((0, 0), (0, 0), (0, -offset), (0, 0), (0, 0)))
    return padded[:, :, -offset:-offset + slot_count]


def band_product(factor_left, factor_right):
    total_rows = factor_left.shape[1]
    slot_count = factor_left.shape[2]
    half_band = slot_count // 2
    padded = jnp.pad(factor_right, ((0, 0), (half_band, half_band), (0, 0), (0, 0), (0, 0)))
    lead_count = max(factor_left.shape[0], factor_right.shape[0])
    total = jnp.zeros((lead_count, total_rows, slot_count, factor_left.shape[3], factor_right.shape[4]), jnp.float32)
    for stride in range(slot_count):
        source = slide_slots(padded[:, stride:stride + total_rows], stride - half_band)
        factor = factor_left[:, :, stride:stride + 1].astype(jnp.float32)
        total = total + jnp.matmul(factor, source.astype(jnp.float32))
    return total


def band_keep(band_pattern):
    total_rows, slot_count = band_pattern.shape
    half_band = slot_count // 2
    row_ids = jnp.arange(total_rows, dtype=jnp.int32)[:, None]
    columns = row_ids + jnp.arange(slot_count, dtype=jnp.int32)[None, :] - half_band
    return (band_pattern == 1) & (columns >= 0) & (columns < total_rows)


def reference(band_pattern, density_in, field_terms, fit_blocks, tensor, metric_inv):
    keep_mask = band_keep(band_pattern)[None, :, :, None, None]
    zero_half = jnp.zeros((), jnp.bfloat16)
    density = jnp.where(keep_mask, density_in[None], zero_half)
    perturbed = jnp.where(keep_mask, field_terms, zero_half)
    density_sq = jnp.where(keep_mask, band_product(density, density), 0.0).astype(jnp.bfloat16)
    first_sum = band_product(density, perturbed) + band_product(perturbed, density)
    first_order = jnp.where(keep_mask, first_sum, 0.0).astype(jnp.bfloat16)
    second = band_product(density_sq, first_order) + band_product(first_order, density_sq)
    response = jnp.where(keep_mask, 2.0 * first_order.astype(jnp.float32) - second, 0.0).astype(jnp.bfloat16)
    fit_pairs = response[:, fit_blocks]
    flat_blocks = fit_pairs.reshape(fit_pairs.shape[0], fit_pairs.shape[1], -1)
    sums_list = []
    for fit_index in range(fit_pairs.shape[1]):
        integrals = tensor[fit_index].reshape(tensor.shape[1], -1)
        sums_list.append(jnp.dot(flat_blocks[:, fit_index], integrals.T, preferred_element_type=jnp.float32))
    fit_sums = jnp.stack(sums_list, 0)
    coefficients = jnp.einsum("fpq,fkq->fkp", metric_inv, fit_sums, precision=lax.Precision.HIGHEST)
    return response, coefficients
```

```python
import functools

import jax
import jax.numpy as jnp
from jax import lax
from jax.experimental import pallas as pl
from jax.experimental.pallas import tpu as pltpu
from jax.sharding import PartitionSpec as P

MESH = pl.DeviceIdType.MESH
BF16 = jnp.bfloat16
F32 = jnp.float32


def ring_kernel(
    sizes,
    pattern, fit_blocks, density_hbm, fields_hbm, tensor_hbm,
    out, sums,
    staged, keep_src, keep, win1, win2, lhs1, lhs2, result,
    integrals, piece, piece_x, piece_y, got_x, got_y, got_c, piece_f, part, parts_z,
    load_sem, in_send, in_recv, keep_send, keep_recv,
    fwd_send, fwd_recv, bwd_send, bwd_recv,
    out_send, out_recv,
    fx_send, fx_recv, fy_send, fy_recv, fc_send, fc_recv,
    z_send, z_recv, g_send, g_recv, h_send, h_recv,
):
    ys, xs, zs, rows, slots = sizes
    half = slots // 2
    blk = 128
    naux = ys * xs * 2
    total_rows = naux * rows
    aux = lax.axis_index("aux")
    z = lax.axis_index("orb")
    core = aux % 2
    col = aux // 2
    x = col % xs
    y = col // xs
    own_lo = half * blk

    def remote(src, dst, ss, rs, to_aux, to_z):
        return pltpu.make_async_remote_copy(
            src_ref=src, dst_ref=dst, send_sem=ss, recv_sem=rs,
            device_id={"aux": to_aux, "orb": to_z}, device_id_type=MESH,
        )

    def landed(ref, sem):
        pltpu.make_async_copy(ref, ref, sem).wait()

    row = col * (2 * zs) + 2 * z + core
    nxt = (row + 1) % total_rows
    prv = (row + total_rows - 1) % total_rows

    def holder(i):
        c = i // (2 * zs)
        q = i % (2 * zs)
        return 2 * c + q % 2, q // 2

    nxt_aux, nxt_z = holder(nxt)
    prv_aux, prv_z = holder(prv)

    load_d = pltpu.make_async_copy(density_hbm.at[:, 0], staged.at[0], load_sem.at[0])
    load_p = [
        pltpu.make_async_copy(fields_hbm.at[k, :, 0], staged.at[1 + k], load_sem.at[1 + k])
        for k in range(2)
    ]
    load_t = pltpu.make_async_copy(tensor_hbm, integrals, load_sem.at[3])
    load_d.start()
    load_p[0].start()
    load_p[1].start()
    load_t.start()

    barrier = pltpu.get_barrier_semaphore()
    greeted = 0

    def greet(a, b):
        pl.semaphore_signal(barrier, inc=1, device_id={"aux": a, "orb": b}, device_id_type=MESH)

    for step in range(1, zs):
        greet(aux, (z + step) % zs)
        greeted += 1
    for step in range(zs):
        greet(2 * col + 1 - core, (z + step) % zs)
        greeted += 1
    for step in range(1, 2 * xs):
        e = (2 * x + core + step) % (2 * xs)
        if xs > 1:
            @pl.when(e // 2 != x)
            def _():
                greet(2 * xs * y + e, z)
    greeted += 2 * (xs - 1)
    for step in range(1, ys):
        greet(2 * (((y + step) % ys) * xs + x) + core, z)
        greeted += 1
    at_top = (z == zs - 1) & (core == 1)
    at_bottom = (z == 0) & (core == 0)

    @pl.when(at_top)
    def _():
        greet(nxt_aux, nxt_z)

    @pl.when(at_bottom)
    def _():
        greet(prv_aux, prv_z)

    first_row = aux * rows
    column = first_row + z - half

    def mask_of(r):
        there = (pattern[r, z] == 1) & (column + r >= 0) & (column + r < total_rows)
        return jnp.where(there, 1, 0)

    for r in range(rows):
        keep_src[r] = jnp.full((8, blk), mask_of(r), jnp.int32)

    load_d.wait()
    for r in range(rows):
        factor = jnp.full((blk, blk), mask_of(r).astype(F32), F32).astype(BF16)
        staged[0, r] = staged[0, r] * factor

    pl.semaphore_wait(barrier, greeted + jnp.where(at_top | at_bottom, 1, 0))

    def dest_of(r):
        return 2 * col + r % 2, (zs // 2) * core + r // 2

    def send_in(mat, r):
        to_aux, to_z = dest_of(r)
        here = (to_aux == aux) & (to_z == z)
        dst = win1.at[mat, z, pl.ds(own_lo, blk)]

        @pl.when(here)
        def _():
            pltpu.make_async_copy(staged.at[mat, r], dst, in_recv.at[mat, z]).start()

        @pl.when(jnp.logical_not(here))
        def _():
            remote(staged.at[mat, r], dst, in_send.at[mat, r], in_recv.at[mat, z], to_aux, to_z).start()

    def send_keep(r):
        to_aux, to_z = dest_of(r)
        here = (to_aux == aux) & (to_z == z)

        @pl.when(here)
        def _():
            pltpu.make_async_copy(keep_src.at[r], keep.at[z], keep_recv.at[z]).start()

        @pl.when(jnp.logical_not(here))
        def _():
            remote(keep_src.at[r], keep.at[z], keep_send.at[r], keep_recv.at[z], to_aux, to_z).start()

    for r in range(rows):
        send_in(0, r)
    for k in range(2):
        load_p[k].wait()
        for r in range(rows):
            factor = jnp.full((blk, blk), mask_of(r).astype(F32), F32).astype(BF16)
            staged[1 + k, r] = staged[1 + k, r] * factor
        for r in range(rows):
            send_in(1 + k, r)
    for r in range(rows):
        send_keep(r)

    for t in range(slots):
        empty = range(t + half, slots) if t < half else range(0, t - half)
        for s in empty:
            for mat in range(3):
                win1[mat, s, pl.ds(t * blk, blk)] = jnp.zeros((blk, blk), BF16)
                win2[mat, s, pl.ds(t * blk, blk)] = jnp.zeros((blk, blk), BF16)

    def forward(win, phase, mat, step):
        t = half + 1 - step
        n = t + half - 1
        return remote(
            win.at[mat, pl.ds(1, n), pl.ds(t * blk, blk)],
            win.at[mat, pl.ds(0, n), pl.ds((t - 1) * blk, blk)],
            fwd_send.at[phase, mat, step - 1], fwd_recv.at[phase, mat, step - 1], nxt_aux, nxt_z,
        )

    def backward(win, phase, mat, step):
        t = half - 1 + step
        n = 2 * slots - half - 1 - t
        return remote(
            win.at[mat, pl.ds(t - half, n), pl.ds(t * blk, blk)],
            win.at[mat, pl.ds(t - half + 1, n), pl.ds((t + 1) * blk, blk)],
            bwd_send.at[phase, mat, step - 1], bwd_recv.at[phase, mat, step - 1], prv_aux, prv_z,
        )

    steps_f, steps_b = half, half - 1

    def advance(win, phase, mat, step):
        if step > 1 and step <= steps_f + 1:
            forward(win, phase, mat, step - 1).wait_recv()
        if step <= steps_f:
            forward(win, phase, mat, step).start()
        if step > 1 and step <= steps_b + 1:
            backward(win, phase, mat, step - 1).wait_recv()
        if step <= steps_b:
            backward(win, phase, mat, step).start()

    def arrived(mat):
        for u in range(slots):
            landed(win1.at[mat, u, pl.ds(own_lo, blk)], in_recv.at[mat, u])
        for u in range(slots):
            lhs1[mat, :, pl.ds(u * blk, blk)] = win1[mat, u, pl.ds(own_lo, blk)]

    def kept(s, value):
        mask = jnp.broadcast_to(keep[s, pl.ds(0, 1), :], (blk, blk))
        return jnp.where(mask > 0, value, 0.0)

    def square():
        def body(s, carry):
            value = jnp.dot(lhs1[0], win1[0, s], preferred_element_type=F32)
            win2[0, s, pl.ds(own_lo, blk)] = kept(s, value).astype(BF16)
            return carry

        lax.fori_loop(0, slots, body, 0)
        for s in range(slots):
            lhs2[0, :, pl.ds(s * blk, blk)] = win2[0, s, pl.ds(own_lo, blk)]

    def first(k):
        def body(s, carry):
            value = jnp.dot(lhs1[0], win1[1 + k, s], preferred_element_type=F32)
            value = value + jnp.dot(lhs1[1 + k], win1[0, s], preferred_element_type=F32)
            win2[1 + k, s, pl.ds(own_lo, blk)] = kept(s, value).astype(BF16)
            return carry

        lax.fori_loop(0, slots, body, 0)
        for s in range(slots):
            lhs2[1 + k, :, pl.ds(s * blk, blk)] = win2[1 + k, s, pl.ds(own_lo, blk)]

    def second(k):
        def body(s, carry):
            value = jnp.dot(lhs2[0], win2[1 + k, s], preferred_element_type=F32)
            value = value + jnp.dot(lhs2[1 + k], win2[0, s], preferred_element_type=F32)
            value = 2.0 * win2[1 + k, s, pl.ds(own_lo, blk)].astype(F32) - value
            result[k, s] = kept(s, value).astype(BF16)
            return carry

        lax.fori_loop(0, slots, body, 0)

    src_aux = 2 * col + z // (zs // 2)
    src_row = (2 * z + core) % rows

    def send_out(k, s):
        here = (src_aux == aux) & (z == s)
        dst = out.at[k, src_row, 0]

        @pl.when(here)
        def _():
            pltpu.make_async_copy(result.at[k, s], dst, out_recv.at[k, src_row]).start()

        @pl.when(jnp.logical_not(here))
        def _():
            remote(result.at[k, s], dst, out_send.at[k, s], out_recv.at[k, src_row], src_aux, s).start()

    done = steps_f + 1
    first_wave = (0, 1, 2, 5, 6, 7)
    for wave in range(first_wave[-1] + done):
        for item in range(6):
            step = wave - first_wave[item] + 1
            if step < 1 or step > done:
                continue
            phase, mat = item // 3, item % 3
            if step == 1 and phase == 0:
                arrived(mat)
            advance(win1 if phase == 0 else win2, phase, mat, step)
            if step == done and phase == 0:
                if mat == 0:
                    for u in range(slots):
                        landed(keep.at[u], keep_recv.at[u])
                    square()
                else:
                    first(mat - 1)
            if step == done and phase == 1 and mat > 0:
                second(mat - 1)
                for s in range(slots):
                    send_out(mat - 1, s)

    for k in range(2):
        for r in range(rows):
            landed(out.at[k, r, 0], out_recv.at[k, r])

    fitted = fit_blocks[0]
    owner = jnp.where(fitted // rows == aux, 1.0, 0.0)
    local_row = fitted % rows
    flag = jnp.full((blk, blk), owner, F32).astype(BF16)
    for k in range(2):
        piece[k] = out[k, local_row, 0] * flag

    def spread(src, got, ss, rs, count, target):
        copies = [
            remote(src, got.at[d - 1], ss.at[d - 1], rs.at[d - 1], target(d), z)
            for d in range(1, count)
        ]
        for c in copies:
            c.start()
        for c in copies:
            c.wait_recv()
        return copies

    pending = spread(
        piece, got_x, fx_send, fx_recv, xs, lambda d: 2 * (y * xs + (x + d) % xs) + core
    )
    for k in range(2):
        value = piece[k]
        for d in range(1, xs):
            value = value + got_x[d - 1, k]
        piece_x[k] = value
    pending += spread(
        piece_x, got_y, fy_send, fy_recv, ys, lambda d: 2 * (((y + d) % ys) * xs + x) + core
    )
    for k in range(2):
        value = piece_x[k]
        for d in range(1, ys):
            value = value + got_y[d - 1, k]
        piece_y[k] = value
    pending += spread(piece_y, got_c, fc_send, fc_recv, 2, lambda d: 2 * col + 1 - core)
    for k in range(2):
        piece_f[k] = (piece_y[k] + got_c[0, k]).astype(F32)

    load_t.wait()
    count_aux = integrals.shape[0]

    def contract(step, carry):
        acc0, acc1 = carry
        base = pl.multiple_of(step * 8, 8)
        rows0 = piece_f[0, pl.ds(base, 8)]
        rows1 = piece_f[1, pl.ds(base, 8)]
        for j in range(8):
            lanes = pl.ds(pl.multiple_of(step * 8 * blk + j * blk, blk), blk)
            slab = integrals[:, lanes].astype(F32)
            acc0 = acc0 + slab * rows0[j : j + 1]
            acc1 = acc1 + slab * rows1[j : j + 1]
        return acc0, acc1

    zero = jnp.zeros((count_aux, blk), F32)
    acc = lax.fori_loop(0, blk // 8, contract, (zero, zero))
    part[...] = jnp.zeros_like(part)
    for k in range(2):
        wide = jnp.concatenate([acc[k], jnp.zeros((blk - count_aux, blk), F32)], axis=0)
        part[pl.ds(k, 1)] = jnp.sum(wide.T, axis=0, keepdims=True)

    parts_z[z] = part[...]
    z_copies = [
        remote(part, parts_z.at[z], z_send.at[d - 1], z_recv.at[d - 1], aux, (z + d) % zs)
        for d in range(1, zs)
    ]
    for c in z_copies:
        c.start()
    for c in z_copies:
        c.wait_recv()
    total = parts_z[0]
    for d in range(1, zs):
        total = total + parts_z[d]
    sums[aux] = total

    group = 2 * xs
    e = 2 * x + core
    g_copies = [
        remote(sums.at[aux], sums.at[aux], g_send.at[d - 1], g_recv.at[d - 1], group * y + (e + d) % group, z)
        for d in range(1, group)
    ]
    for c in g_copies:
        c.start()
    for c in g_copies:
        c.wait_recv()
    mine = sums.at[pl.ds(group * y, group)]
    h_copies = [
        remote(mine, mine, h_send.at[d - 1], h_recv.at[d - 1], 2 * (((y + d) % ys) * xs + x) + core, z)
        for d in range(1, ys)
    ]
    for c in h_copies:
        c.start()
    for c in h_copies:
        c.wait_recv()

    for c in pending + z_copies + g_copies + h_copies:
        c.wait_send()
    for r in range(rows):
        to_aux, to_z = dest_of(r)

        @pl.when(jnp.logical_not((to_aux == aux) & (to_z == z)))
        def _():
            for mat in range(3):
                dst = win1.at[mat, z, pl.ds(own_lo, blk)]
                remote(staged.at[mat, r], dst, in_send.at[mat, r], in_recv.at[mat, z], to_aux, to_z).wait_send()
            remote(keep_src.at[r], keep.at[z], keep_send.at[r], keep_recv.at[z], to_aux, to_z).wait_send()
    for s in range(slots):
        @pl.when(jnp.logical_not((src_aux == aux) & (z == s)))
        def _():
            for k in range(2):
                remote(
                    result.at[k, s], out.at[k, src_row, 0], out_send.at[k, s], out_recv.at[k, src_row], src_aux, s
                ).wait_send()
    for phase, win in enumerate((win1, win2)):
        for mat in range(3):
            for step in range(1, steps_f + 1):
                forward(win, phase, mat, step).wait_send()
            for step in range(1, steps_b + 1):
                backward(win, phase, mat, step).wait_send()


def solution(mesh):
    naux, zs = mesh.shape["aux"], mesh.shape["orb"]
    side = {32: (4, 4), 8: (2, 2), 2: (1, 1)}[naux]
    ys, xs = side

    def on_device(band_pattern, density_in, field_terms, fit_blocks, tensor, metric_inv):
        rows = density_in.shape[0]
        slots = zs
        blk = density_in.shape[2]
        count_aux = tensor.shape[1]
        dma = pltpu.SemaphoreType.DMA
        vmem = pltpu.VMEM
        block = (blk, blk)
        half = slots // 2
        in_hbm = pl.BlockSpec(memory_space=pltpu.HBM)
        smem = pl.BlockSpec(memory_space=pltpu.SMEM)
        in_vmem = pl.BlockSpec(memory_space=pltpu.VMEM)
        response, sums = pl.pallas_call(
            functools.partial(ring_kernel, (ys, xs, zs, rows, slots)),
            out_shape=(
                jax.ShapeDtypeStruct(field_terms.shape, BF16),
                jax.ShapeDtypeStruct((naux, 8, blk), F32),
            ),
            in_specs=[smem, smem, in_hbm, in_hbm, in_hbm],
            out_specs=(in_vmem, in_vmem),
            scratch_shapes=[
                vmem((3, rows, *block), BF16),
                vmem((rows, 8, blk), jnp.int32),
                vmem((slots, 8, blk), jnp.int32),
                vmem((3, slots, slots * blk, blk), BF16),
                vmem((3, slots, slots * blk, blk), BF16),
                vmem((3, blk, slots * blk), BF16),
                vmem((3, blk, slots * blk), BF16),
                vmem((2, slots, *block), BF16),
                vmem((count_aux, blk * blk), BF16),
                vmem((2, *block), BF16),
                vmem((2, *block), BF16),
                vmem((2, *block), BF16),
                vmem((max(xs - 1, 1), 2, *block), BF16),
                vmem((max(ys - 1, 1), 2, *block), BF16),
                vmem((1, 2, *block), BF16),
                vmem((2, *block), F32),
                vmem((8, blk), F32),
                vmem((zs, 8, blk), F32),
                dma((4,)),
                dma((3, rows)), dma((3, slots)),
                dma((rows,)), dma((slots,)),
                dma((2, 3, half)), dma((2, 3, half)),
                dma((2, 3, half)), dma((2, 3, half)),
                dma((2, slots)), dma((2, rows)),
                dma((max(xs - 1, 1),)), dma((max(xs - 1, 1),)),
                dma((max(ys - 1, 1),)), dma((max(ys - 1, 1),)),
                dma((1,)), dma((1,)),
                dma((zs,)), dma((zs,)),
                dma((2 * xs,)), dma((2 * xs,)),
                dma((max(ys - 1, 1),)), dma((max(ys - 1, 1),)),
            ],
            compiler_params=pltpu.CompilerParams(
                collective_id=0, has_side_effects=True, vmem_limit_bytes=48 << 20
            ),
        )(
            band_pattern, fit_blocks, density_in, field_terms,
            tensor.reshape(count_aux, blk * blk),
        )
        full = sums[:, :2, :count_aux].transpose(1, 0, 2).reshape(1, 2, naux * count_aux)
        coefficients = jnp.einsum("fpq,fkq->fkp", metric_inv, full, precision=lax.Precision.HIGHEST)
        return response, coefficients

    in_specs = (
        P("aux", None),
        P("aux", "orb", None, None),
        P(None, "aux", "orb", None, None),
        P(),
        P(None, "aux", "orb", None),
        P(None, "aux", None),
    )
    out_specs = (P(None, "aux", "orb", None, None), P(None, None, "aux"))
    return jax.shard_map(
        on_device, mesh=mesh, in_specs=in_specs, out_specs=out_specs, check_vma=False
    )
```

```python
import functools

import jax
import jax.numpy as jnp
from jax import lax
from jax.experimental import pallas as pl
from jax.experimental.pallas import tpu as pltpu
from jax.sharding import PartitionSpec as P

MESH = pl.DeviceIdType.MESH
BF16 = jnp.bfloat16
F32 = jnp.float32


def ring_kernel(
    sizes,
    pattern, fit_blocks, density_hbm, fields_hbm, tensor_hbm,
    out, sums,
    staged, keep_src, keep, win1, win2, lhs1, lhs2, result,
    integrals, piece, piece_x, piece_y, got_x, got_y, got_c, piece_f, part, parts_z,
    load_sem, in_send, in_recv, keep_send, keep_recv,
    win_send, win_recv,
    out_send, out_recv,
    fx_send, fx_recv, fy_send, fy_recv, fc_send, fc_recv,
    z_send, z_recv, g_send, g_recv, h_send, h_recv,
):
    ys, xs, zs, rows, slots = sizes
    half = slots // 2
    blk = 128
    naux = ys * xs * 2
    total_rows = naux * rows
    aux = lax.axis_index("aux")
    z = lax.axis_index("orb")
    core = aux % 2
    col = aux // 2
    x = col % xs
    y = col // xs
    own_lo = half * blk

    def remote(src, dst, ss, rs, to_aux, to_z):
        return pltpu.make_async_remote_copy(
            src_ref=src, dst_ref=dst, send_sem=ss, recv_sem=rs,
            device_id={"aux": to_aux, "orb": to_z}, device_id_type=MESH,
        )

    def landed(ref, sem):
        pltpu.make_async_copy(ref, ref, sem).wait()

    row = 2 * xs * zs * y + 2 * (z * xs + x) + core

    def holder(i):
        i = (i + total_rows) % total_rows
        pair = (i % (2 * xs * zs)) // 2
        return 2 * (i // (2 * xs * zs) * xs + pair % xs) + i % 2, pair // xs

    def dest_of(r):
        return holder(aux * rows + r)

    src_aux, src_row = row // rows, row % rows

    load_d = pltpu.make_async_copy(density_hbm.at[:, 0], staged.at[0], load_sem.at[0])
    load_p = [
        pltpu.make_async_copy(fields_hbm.at[k, :, 0], staged.at[1 + k], load_sem.at[1 + k])
        for k in range(2)
    ]
    load_t = pltpu.make_async_copy(tensor_hbm, integrals, load_sem.at[3])
    load_d.start()
    load_p[0].start()
    load_p[1].start()
    load_t.start()

    barrier = pltpu.get_barrier_semaphore()
    greeted = 0

    def greet(a, b):
        pl.semaphore_signal(barrier, inc=1, device_id={"aux": a, "orb": b}, device_id_type=MESH)

    self_holds = src_aux == aux
    for r in range(rows):
        to_aux, to_z = dest_of(r)

        @pl.when(jnp.logical_not((to_aux == aux) & (to_z == z)))
        def _():
            greet(to_aux, to_z)

    for s in range(zs):
        @pl.when(jnp.logical_not((src_aux == aux) & (z == s)))
        def _():
            greet(src_aux, s)

    greeted += rows + zs
    for offset in (-2, -1, 1, 2):
        greet(*holder(row + offset))
    greeted += 4
    for step in range(1, zs):
        greet(aux, (z + step) % zs)
    greeted += zs - 1
    for step in range(1, 2 * xs):
        greet(2 * xs * y + (2 * x + core + step) % (2 * xs), z)
    greeted += 2 * xs - 1
    for step in range(1, ys):
        greet(2 * (((y + step) % ys) * xs + x) + core, z)
        greeted += 1

    first_row = aux * rows
    column = first_row + z - half

    def mask_of(r):
        there = (pattern[r, z] == 1) & (column + r >= 0) & (column + r < total_rows)
        return jnp.where(there, 1, 0)

    for r in range(rows):
        keep_src[r] = jnp.full((8, blk), mask_of(r), jnp.int32)

    load_d.wait()
    for r in range(rows):
        factor = jnp.full((blk, blk), mask_of(r).astype(F32), F32).astype(BF16)
        staged[0, r] = staged[0, r] * factor

    pl.semaphore_wait(barrier, greeted - jnp.where(self_holds, 2, 0))

    def send_in(mat, r):
        to_aux, to_z = dest_of(r)
        here = (to_aux == aux) & (to_z == z)
        dst = win1.at[mat, z, pl.ds(own_lo, blk)]

        @pl.when(here)
        def _():
            pltpu.make_async_copy(staged.at[mat, r], dst, in_recv.at[mat, z]).start()

        @pl.when(jnp.logical_not(here))
        def _():
            remote(staged.at[mat, r], dst, in_send.at[mat, r], in_recv.at[mat, z], to_aux, to_z).start()

    def send_keep(r):
        to_aux, to_z = dest_of(r)
        here = (to_aux == aux) & (to_z == z)

        @pl.when(here)
        def _():
            pltpu.make_async_copy(keep_src.at[r], keep.at[z], keep_recv.at[z]).start()

        @pl.when(jnp.logical_not(here))
        def _():
            remote(keep_src.at[r], keep.at[z], keep_send.at[r], keep_recv.at[z], to_aux, to_z).start()

    for r in range(rows):
        send_in(0, r)
    for r in range(rows):
        send_keep(r)
    for k in range(2):
        load_p[k].wait()
        for r in range(rows):
            factor = jnp.full((blk, blk), mask_of(r).astype(F32), F32).astype(BF16)
            staged[1 + k, r] = staged[1 + k, r] * factor
        for r in range(rows):
            send_in(1 + k, r)

    for t in range(slots):
        empty = range(t + half, slots) if t < half else range(0, t - half)
        for s in empty:
            for mat in range(3):
                win1[mat, s, pl.ds(t * blk, blk)] = jnp.zeros((blk, blk), BF16)
                win2[mat, s, pl.ds(t * blk, blk)] = jnp.zeros((blk, blk), BF16)

    def slots_of(t):
        return max(0, t - half), min(slots, t + half)

    def message(win, phase, mat, index, t, offset):
        to = t - offset
        lo, hi = slots_of(to)
        to_aux, to_z = holder(row + offset)
        return remote(
            win.at[mat, pl.ds(lo + offset, hi - lo), pl.ds(t * blk, blk)],
            win.at[mat, pl.ds(lo, hi - lo), pl.ds(to * blk, blk)],
            win_send.at[phase, mat, index], win_recv.at[phase, mat, to], to_aux, to_z,
        )

    def got(win, phase, mat, t):
        lo, hi = slots_of(t)
        landed(win.at[mat, pl.ds(lo, hi - lo), pl.ds(t * blk, blk)], win_recv.at[phase, mat, t])

    plan = (
        (
            ((), ((half, 2), (half, -1), (half, 1))),
            ((3, 2), ((3, 2), (2, 2), (3, 1), (2, 1))),
            ((1, 0), ((1, 1),)),
            ((5, 6, 7), ()),
        ),
        (
            ((), ((half, 1), (half, -2), (half, -1))),
            ((5, 6), ((5, -2), (5, -1), (6, -1))),
            ((7,), ()),
            ((3, 2, 1, 0), ()),
        ),
    )

    def advance(win, phase, mat, step):
        for c in range(2):
            @pl.when(core == c)
            def _():
                waits, sends = plan[c][step - 1]
                index = sum(len(plan[c][j][1]) for j in range(step - 1))
                for t in waits:
                    got(win, phase, mat, t)
                for t, offset in sends:
                    message(win, phase, mat, index, t, offset).start()
                    index += 1

    def arrived(mat):
        for u in range(slots):
            landed(win1.at[mat, u, pl.ds(own_lo, blk)], in_recv.at[mat, u])
        for u in range(slots):
            lhs1[mat, :, pl.ds(u * blk, blk)] = win1[mat, u, pl.ds(own_lo, blk)]

    def kept(s, value):
        mask = jnp.broadcast_to(keep[s, pl.ds(0, 1), :], (blk, blk))
        return jnp.where(mask > 0, value, 0.0)

    def square():
        def body(s, carry):
            value = jnp.dot(lhs1[0], win1[0, s], preferred_element_type=F32)
            win2[0, s, pl.ds(own_lo, blk)] = kept(s, value).astype(BF16)
            return carry

        lax.fori_loop(0, slots, body, 0)
        for s in range(slots):
            lhs2[0, :, pl.ds(s * blk, blk)] = win2[0, s, pl.ds(own_lo, blk)]

    def first(k):
        def body(s, carry):
            value = jnp.dot(lhs1[0], win1[1 + k, s], preferred_element_type=F32)
            value = value + jnp.dot(lhs1[1 + k], win1[0, s], preferred_element_type=F32)
            win2[1 + k, s, pl.ds(own_lo, blk)] = kept(s, value).astype(BF16)
            return carry

        lax.fori_loop(0, slots, body, 0)
        for s in range(slots):
            lhs2[1 + k, :, pl.ds(s * blk, blk)] = win2[1 + k, s, pl.ds(own_lo, blk)]

    def second(k):
        def body(s, carry):
            value = jnp.dot(lhs2[0], win2[1 + k, s], preferred_element_type=F32)
            value = value + jnp.dot(lhs2[1 + k], win2[0, s], preferred_element_type=F32)
            value = 2.0 * win2[1 + k, s, pl.ds(own_lo, blk)].astype(F32) - value
            result[k, s] = kept(s, value).astype(BF16)
            return carry

        lax.fori_loop(0, slots, body, 0)

    def send_out(k, s):
        here = (src_aux == aux) & (z == s)
        dst = out.at[k, src_row, 0]

        @pl.when(here)
        def _():
            pltpu.make_async_copy(result.at[k, s], dst, out_recv.at[k, src_row]).start()

        @pl.when(jnp.logical_not(here))
        def _():
            remote(result.at[k, s], dst, out_send.at[k, s], out_recv.at[k, src_row], src_aux, s).start()

    done = 4
    first_wave = (0, 1, 2, 3, 4, 5)
    for wave in range(first_wave[-1] + done):
        for item in range(6):
            step = wave - first_wave[item] + 1
            if step < 1 or step > done:
                continue
            phase, mat = item // 3, item % 3
            if step == 1 and phase == 0:
                arrived(mat)
            if step == 1 and phase == 1:
                if mat == 0:
                    for u in range(slots):
                        landed(keep.at[u], keep_recv.at[u])
                    square()
                else:
                    first(mat - 1)
            advance(win1 if phase == 0 else win2, phase, mat, step)
            if step == done and phase == 1 and mat > 0:
                second(mat - 1)
                for s in range(slots):
                    send_out(mat - 1, s)

    for k in range(2):
        for r in range(rows):
            landed(out.at[k, r, 0], out_recv.at[k, r])

    fitted = fit_blocks[0]
    owner = jnp.where(fitted // rows == aux, 1.0, 0.0)
    local_row = fitted % rows
    flag = jnp.full((blk, blk), owner, F32).astype(BF16)
    for k in range(2):
        piece[k] = out[k, local_row, 0] * flag

    def over_x(d):
        return 2 * (y * xs + (x + d) % xs) + core

    def over_y(d):
        return 2 * (((y + d) % ys) * xs + x) + core

    pending = []

    def spread(src, got_there, count, ss, rs, target):
        copies = [
            remote(src, got_there.at[d - 1], ss.at[d - 1], rs.at[d - 1], target(d), z)
            for d in range(1, count)
        ]
        for c in copies:
            c.start()
        pending.extend(copies)
        return copies

    def added(src, got_there, copies):
        value = src[...]
        for d, c in enumerate(copies):
            c.wait_recv()
            value = value + got_there[d]
        return value

    first_x = spread(piece.at[0], got_x.at[0], xs, fx_send.at[0], fx_recv.at[0], over_x)
    first_y = spread(piece.at[1], got_y.at[0], ys, fy_send.at[0], fy_recv.at[0], over_y)
    piece_x[0] = added(piece.at[0], got_x.at[0], first_x)
    then_y = spread(piece_x.at[0], got_y.at[1], ys, fy_send.at[1], fy_recv.at[1], over_y)
    piece_x[1] = added(piece.at[1], got_y.at[0], first_y)
    then_x = spread(piece_x.at[1], got_x.at[1], xs, fx_send.at[1], fx_recv.at[1], over_x)
    piece_y[0] = added(piece_x.at[0], got_y.at[1], then_y)
    over0 = spread(piece_y.at[0], got_c.at[0], 2, fc_send.at[0], fc_recv.at[0], lambda d: aux + 1 - 2 * core)
    piece_y[1] = added(piece_x.at[1], got_x.at[1], then_x)
    over1 = spread(piece_y.at[1], got_c.at[1], 2, fc_send.at[1], fc_recv.at[1], lambda d: aux + 1 - 2 * core)
    piece_f[0] = added(piece_y.at[0], got_c.at[0], over0).astype(F32)
    piece_f[1] = added(piece_y.at[1], got_c.at[1], over1).astype(F32)

    load_t.wait()
    count_aux = integrals.shape[0]

    def contract(step, carry):
        acc0, acc1 = carry
        base = pl.multiple_of(step * 8, 8)
        rows0 = piece_f[0, pl.ds(base, 8)]
        rows1 = piece_f[1, pl.ds(base, 8)]
        for j in range(8):
            lanes = pl.ds(pl.multiple_of(step * 8 * blk + j * blk, blk), blk)
            slab = integrals[:, lanes].astype(F32)
            acc0 = acc0 + slab * rows0[j : j + 1]
            acc1 = acc1 + slab * rows1[j : j + 1]
        return acc0, acc1

    zero = jnp.zeros((count_aux, blk), F32)
    acc = lax.fori_loop(0, blk // 8, contract, (zero, zero))
    part[...] = jnp.zeros_like(part)
    for k in range(2):
        wide = jnp.concatenate([acc[k], jnp.zeros((blk - count_aux, blk), F32)], axis=0)
        part[pl.ds(k, 1)] = jnp.sum(wide.T, axis=0, keepdims=True)

    parts_z[z] = part[...]
    z_copies = [
        remote(part, parts_z.at[z], z_send.at[d - 1], z_recv.at[d - 1], aux, (z + d) % zs)
        for d in range(1, zs)
    ]
    for c in z_copies:
        c.start()
    for c in z_copies:
        c.wait_recv()
    total = parts_z[0]
    for d in range(1, zs):
        total = total + parts_z[d]
    sums[aux] = total

    group = 2 * xs
    e = 2 * x + core
    g_copies = [
        remote(sums.at[aux], sums.at[aux], g_send.at[d - 1], g_recv.at[d - 1], group * y + (e + d) % group, z)
        for d in range(1, group)
    ]
    for c in g_copies:
        c.start()
    for c in g_copies:
        c.wait_recv()
    mine = sums.at[pl.ds(group * y, group)]
    h_copies = [
        remote(mine, mine, h_send.at[d - 1], h_recv.at[d - 1], 2 * (((y + d) % ys) * xs + x) + core, z)
        for d in range(1, ys)
    ]
    for c in h_copies:
        c.start()
    for c in h_copies:
        c.wait_recv()

    for c in pending + z_copies + g_copies + h_copies:
        c.wait_send()
    for r in range(rows):
        to_aux, to_z = dest_of(r)

        @pl.when(jnp.logical_not((to_aux == aux) & (to_z == z)))
        def _():
            for mat in range(3):
                dst = win1.at[mat, z, pl.ds(own_lo, blk)]
                remote(staged.at[mat, r], dst, in_send.at[mat, r], in_recv.at[mat, z], to_aux, to_z).wait_send()
            remote(keep_src.at[r], keep.at[z], keep_send.at[r], keep_recv.at[z], to_aux, to_z).wait_send()
    for s in range(slots):
        @pl.when(jnp.logical_not((src_aux == aux) & (z == s)))
        def _():
            for k in range(2):
                remote(
                    result.at[k, s], out.at[k, src_row, 0], out_send.at[k, s], out_recv.at[k, src_row], src_aux, s
                ).wait_send()
    for c in range(2):
        @pl.when(core == c)
        def _():
            sends = [one for stage in plan[c] for one in stage[1]]
            for phase, win in enumerate((win1, win2)):
                for mat in range(3):
                    for index, (t, offset) in enumerate(sends):
                        message(win, phase, mat, index, t, offset).wait_send()


def solution(mesh):
    naux, zs = mesh.shape["aux"], mesh.shape["orb"]
    side = {32: (4, 4), 8: (2, 2), 4: (1, 2), 2: (1, 1)}[naux]
    ys, xs = side

    def on_device(band_pattern, density_in, field_terms, fit_blocks, tensor, metric_inv):
        rows = density_in.shape[0]
        slots = zs
        blk = density_in.shape[2]
        count_aux = tensor.shape[1]
        dma = pltpu.SemaphoreType.DMA
        vmem = pltpu.VMEM
        block = (blk, blk)
        in_hbm = pl.BlockSpec(memory_space=pltpu.HBM)
        smem = pl.BlockSpec(memory_space=pltpu.SMEM)
        in_vmem = pl.BlockSpec(memory_space=pltpu.VMEM)
        response, sums = pl.pallas_call(
            functools.partial(ring_kernel, (ys, xs, zs, rows, slots)),
            out_shape=(
                jax.ShapeDtypeStruct(field_terms.shape, BF16),
                jax.ShapeDtypeStruct((naux, 8, blk), F32),
            ),
            in_specs=[smem, smem, in_hbm, in_hbm, in_hbm],
            out_specs=(in_vmem, in_vmem),
            scratch_shapes=[
                vmem((3, rows, *block), BF16),
                vmem((rows, 8, blk), jnp.int32),
                vmem((slots, 8, blk), jnp.int32),
                vmem((3, slots, slots * blk, blk), BF16),
                vmem((3, slots, slots * blk, blk), BF16),
                vmem((3, blk, slots * blk), BF16),
                vmem((3, blk, slots * blk), BF16),
                vmem((2, slots, *block), BF16),
                vmem((count_aux, blk * blk), BF16),
                vmem((2, *block), BF16),
                vmem((2, *block), BF16),
                vmem((2, *block), BF16),
                vmem((2, max(xs - 1, 1), *block), BF16),
                vmem((2, max(ys - 1, 1), *block), BF16),
                vmem((2, 1, *block), BF16),
                vmem((2, *block), F32),
                vmem((8, blk), F32),
                vmem((zs, 8, blk), F32),
                dma((4,)),
                dma((3, rows)), dma((3, slots)),
                dma((rows,)), dma((slots,)),
                dma((2, 3, slots)), dma((2, 3, slots)),
                dma((2, slots)), dma((2, rows)),
                dma((2, max(xs - 1, 1))), dma((2, max(xs - 1, 1))),
                dma((2, max(ys - 1, 1))), dma((2, max(ys - 1, 1))),
                dma((2, 1)), dma((2, 1)),
                dma((zs,)), dma((zs,)),
                dma((2 * xs,)), dma((2 * xs,)),
                dma((max(ys - 1, 1),)), dma((max(ys - 1, 1),)),
            ],
            compiler_params=pltpu.CompilerParams(
                collective_id=0, has_side_effects=True, vmem_limit_bytes=62 << 20
            ),
        )(
            band_pattern, fit_blocks, density_in, field_terms,
            tensor.reshape(count_aux, blk * blk),
        )
        full = sums[:, :2, :count_aux].transpose(1, 0, 2).reshape(1, 2, naux * count_aux)
        coefficients = jnp.einsum("fpq,fkq->fkp", metric_inv, full, precision=lax.Precision.HIGHEST)
        return response, coefficients

    in_specs = (
        P("aux", None),
        P("aux", "orb", None, None),
        P(None, "aux", "orb", None, None),
        P(),
        P(None, "aux", "orb", None),
        P(None, "aux", None),
    )
    out_specs = (P(None, "aux", "orb", None, None), P(None, None, "aux"))
    return jax.shard_map(
        on_device, mesh=mesh, in_specs=in_specs, out_specs=out_specs, check_vma=False
    )
```

```python
import functools

import jax
import jax.numpy as jnp
from jax import lax
from jax.experimental import pallas as pl
from jax.experimental.pallas import tpu as pltpu
from jax.sharding import PartitionSpec as P

MESH = pl.DeviceIdType.MESH
BF16 = jnp.bfloat16
F32 = jnp.float32


def ring_kernel(
    sizes,
    pattern, fit_blocks, density_hbm, fields_hbm, tensor_hbm, metric_hbm,
    out, coefficients, sums, metric,
    staged, keep_src, keep, win1, win2, lhs1, lhs2, result,
    integrals, piece, piece_x, piece_y, got_x, got_y, got_c, piece_f, part, parts_z,
    load_sem, in_send, in_recv, keep_send, keep_recv,
    win_send, win_recv,
    out_send, out_recv,
    fx_send, fx_recv, fy_send, fy_recv, fc_send, fc_recv,
    z_send, z_recv, g_send, g_recv, h_send, h_recv,
):
    ys, xs, zs, rows, slots = sizes
    half = slots // 2
    blk = 128
    naux = ys * xs * 2
    total_rows = naux * rows
    aux = lax.axis_index("aux")
    z = lax.axis_index("orb")
    core = aux % 2
    col = aux // 2
    x = col % xs
    y = col // xs
    own_lo = half * blk

    def remote(src, dst, ss, rs, to_aux, to_z):
        return pltpu.make_async_remote_copy(
            src_ref=src, dst_ref=dst, send_sem=ss, recv_sem=rs,
            device_id={"aux": to_aux, "orb": to_z}, device_id_type=MESH,
        )

    def landed(ref, sem):
        pltpu.make_async_copy(ref, ref, sem).wait()

    row = 2 * zs * col + 2 * (z + col % 2 * (zs - 1 - 2 * z)) + core

    def holder(i):
        i = (i + total_rows) % total_rows
        q = (i % (2 * zs)) // 2
        c = i // (2 * zs)
        return 2 * c + i % 2, q + c % 2 * (zs - 1 - 2 * q)

    def dest_of(r):
        return holder(aux * rows + r)

    src_aux, src_row = row // rows, row % rows

    load_d = pltpu.make_async_copy(density_hbm.at[:, 0], staged.at[0], load_sem.at[0])
    load_p = [
        pltpu.make_async_copy(fields_hbm.at[k, :, 0], staged.at[1 + k], load_sem.at[1 + k])
        for k in range(2)
    ]
    load_t = pltpu.make_async_copy(tensor_hbm, integrals, load_sem.at[3])
    load_d.start()
    load_p[0].start()
    load_p[1].start()
    load_t.start()
    load_m = pltpu.make_async_copy(metric_hbm.at[0], metric, load_sem.at[4])
    load_m.start()

    barrier = pltpu.get_barrier_semaphore()
    greeted = 0

    def greet(a, b):
        pl.semaphore_signal(barrier, inc=1, device_id={"aux": a, "orb": b}, device_id_type=MESH)

    self_holds = src_aux == aux
    for r in range(rows):
        to_aux, to_z = dest_of(r)

        @pl.when(jnp.logical_not((to_aux == aux) & (to_z == z)))
        def _():
            greet(to_aux, to_z)

    for s in range(zs):
        @pl.when(jnp.logical_not((src_aux == aux) & (z == s)))
        def _():
            greet(src_aux, s)

    greeted += rows + zs
    for offset in (-2, -1, 1, 2):
        greet(*holder(row + offset))
    greeted += 4
    for step in range(1, zs):
        greet(aux, (z + step) % zs)
    greeted += zs - 1
    for step in range(1, 2 * xs):
        greet(2 * xs * y + (2 * x + core + step) % (2 * xs), z)
    greeted += 2 * xs - 1
    for step in range(1, ys):
        greet(2 * (((y + step) % ys) * xs + x) + core, z)
        greeted += 1

    first_row = aux * rows
    column = first_row + z - half

    def mask_of(r):
        there = (pattern[r, z] == 1) & (column + r >= 0) & (column + r < total_rows)
        return jnp.where(there, 1, 0)

    for r in range(rows):
        keep_src[r] = jnp.full((8, blk), mask_of(r), jnp.int32)

    load_d.wait()
    for r in range(rows):
        factor = jnp.full((blk, blk), mask_of(r).astype(F32), F32).astype(BF16)
        staged[0, r] = staged[0, r] * factor

    pl.semaphore_wait(barrier, greeted - jnp.where(self_holds, 2, 0))

    def send_in(mat, r):
        to_aux, to_z = dest_of(r)
        here = (to_aux == aux) & (to_z == z)
        dst = win1.at[mat, z, pl.ds(own_lo, blk)]

        @pl.when(here)
        def _():
            pltpu.make_async_copy(staged.at[mat, r], dst, in_recv.at[mat, z]).start()

        @pl.when(jnp.logical_not(here))
        def _():
            remote(staged.at[mat, r], dst, in_send.at[mat, r], in_recv.at[mat, z], to_aux, to_z).start()

    def send_keep(r):
        to_aux, to_z = dest_of(r)
        here = (to_aux == aux) & (to_z == z)

        @pl.when(here)
        def _():
            pltpu.make_async_copy(keep_src.at[r], keep.at[z], keep_recv.at[z]).start()

        @pl.when(jnp.logical_not(here))
        def _():
            remote(keep_src.at[r], keep.at[z], keep_send.at[r], keep_recv.at[z], to_aux, to_z).start()

    for r in range(rows):
        send_in(0, r)
    for r in range(rows):
        send_keep(r)
    for k in range(2):
        load_p[k].wait()
        for r in range(rows):
            factor = jnp.full((blk, blk), mask_of(r).astype(F32), F32).astype(BF16)
            staged[1 + k, r] = staged[1 + k, r] * factor
        for r in range(rows):
            send_in(1 + k, r)

    for t in range(slots):
        empty = range(t + half, slots) if t < half else range(0, t - half)
        for s in empty:
            for mat in range(3):
                win1[mat, s, pl.ds(t * blk, blk)] = jnp.zeros((blk, blk), BF16)
                win2[mat, s, pl.ds(t * blk, blk)] = jnp.zeros((blk, blk), BF16)

    def slots_of(t):
        return max(0, t - half), min(slots, t + half)

    def message(win, phase, mat, index, t, offset):
        to = t - offset
        lo, hi = slots_of(to)
        to_aux, to_z = holder(row + offset)
        return remote(
            win.at[mat, pl.ds(lo + offset, hi - lo), pl.ds(t * blk, blk)],
            win.at[mat, pl.ds(lo, hi - lo), pl.ds(to * blk, blk)],
            win_send.at[phase, mat, index], win_recv.at[phase, mat, to], to_aux, to_z,
        )

    def got(win, phase, mat, t):
        lo, hi = slots_of(t)
        landed(win.at[mat, pl.ds(lo, hi - lo), pl.ds(t * blk, blk)], win_recv.at[phase, mat, t])

    plan = (
        (
            ((), ((half, 2), (half, -1), (half, 1))),
            ((3, 2), ((3, 2), (2, 2), (3, 1), (2, 1))),
            ((1, 0), ((1, 1),)),
            ((5, 6, 7), ()),
        ),
        (
            ((), ((half, 1), (half, -2), (half, -1))),
            ((5, 6), ((5, -2), (5, -1), (6, -1))),
            ((7,), ()),
            ((3, 2, 1, 0), ()),
        ),
    )

    def advance(win, phase, mat, step):
        for c in range(2):
            @pl.when(core == c)
            def _():
                waits, sends = plan[c][step - 1]
                index = sum(len(plan[c][j][1]) for j in range(step - 1))
                for t in waits:
                    got(win, phase, mat, t)
                for t, offset in sends:
                    message(win, phase, mat, index, t, offset).start()
                    index += 1

    def arrived(mat):
        for u in range(slots):
            landed(win1.at[mat, u, pl.ds(own_lo, blk)], in_recv.at[mat, u])
        for u in range(slots):
            lhs1[mat, :, pl.ds(u * blk, blk)] = win1[mat, u, pl.ds(own_lo, blk)]

    def kept(s, value):
        mask = jnp.broadcast_to(keep[s, pl.ds(0, 1), :], (blk, blk))
        return jnp.where(mask > 0, value, 0.0)

    def square():
        def body(s, carry):
            value = jnp.dot(lhs1[0], win1[0, s], preferred_element_type=F32)
            win2[0, s, pl.ds(own_lo, blk)] = kept(s, value).astype(BF16)
            return carry

        lax.fori_loop(0, slots, body, 0)
        for s in range(slots):
            lhs2[0, :, pl.ds(s * blk, blk)] = win2[0, s, pl.ds(own_lo, blk)]

    def first(k):
        def body(s, carry):
            value = jnp.dot(lhs1[0], win1[1 + k, s], preferred_element_type=F32)
            value = value + jnp.dot(lhs1[1 + k], win1[0, s], preferred_element_type=F32)
            win2[1 + k, s, pl.ds(own_lo, blk)] = kept(s, value).astype(BF16)
            return carry

        lax.fori_loop(0, slots, body, 0)
        for s in range(slots):
            lhs2[1 + k, :, pl.ds(s * blk, blk)] = win2[1 + k, s, pl.ds(own_lo, blk)]

    def send_out(k, s):
        here = (src_aux == aux) & (z == s)
        dst = out.at[k, src_row, 0]

        @pl.when(here)
        def _():
            pltpu.make_async_copy(result.at[k, s], dst, out_recv.at[k, src_row]).start()

        @pl.when(jnp.logical_not(here))
        def _():
            remote(result.at[k, s], dst, out_send.at[k, s], out_recv.at[k, src_row], src_aux, s).start()

    def second(k):
        def body(s, carry):
            value = jnp.dot(lhs2[0], win2[1 + k, s], preferred_element_type=F32)
            value = value + jnp.dot(lhs2[1 + k], win2[0, s], preferred_element_type=F32)
            value = 2.0 * win2[1 + k, s, pl.ds(own_lo, blk)].astype(F32) - value
            result[k, s] = kept(s, value).astype(BF16)
            send_out(k, s)
            return carry

        lax.fori_loop(0, slots, body, 0)

    done = 4
    first_wave = (0, 1, 2, 3, 4, 5)
    for wave in range(first_wave[-1] + done):
        for item in range(6):
            step = wave - first_wave[item] + 1
            if step < 1 or step > done:
                continue
            phase, mat = item // 3, item % 3
            if step == 1 and phase == 0:
                arrived(mat)
            if step == 1 and phase == 1:
                if mat == 0:
                    for u in range(slots):
                        landed(keep.at[u], keep_recv.at[u])
                    square()
                else:
                    first(mat - 1)
            advance(win1 if phase == 0 else win2, phase, mat, step)
            if step == done and phase == 1 and mat > 0:
                second(mat - 1)

    fitted = fit_blocks[0]

    def over_x(d):
        return 2 * (y * xs + (x + d) % xs) + core

    def over_y(d):
        return 2 * (((y + d) % ys) * xs + x) + core

    pending = []

    def spread(src, got_there, count, ss, rs, target):
        copies = [
            remote(src, got_there.at[d - 1], ss.at[d - 1], rs.at[d - 1], target(d), z)
            for d in range(1, count)
        ]
        for c in copies:
            c.start()
        pending.extend(copies)
        return copies

    def added(src, got_there, copies):
        value = src[...]
        for d, c in enumerate(copies):
            c.wait_recv()
            value = value + got_there[d]
        return value

    def piece_of(k):
        for r in range(rows):
            landed(out.at[k, r, 0], out_recv.at[k, r])
        value = jnp.zeros((blk, blk), BF16)
        for r in range(rows):
            chosen = jnp.where(fitted == first_row + r, 1.0, 0.0)
            value = value + out[k, r, 0] * jnp.full((blk, blk), chosen, F32).astype(BF16)
        piece[k] = value

    def other_core(d):
        return aux + 1 - 2 * core

    count_aux = integrals.shape[0]

    def contract(k):
        def body(step, acc):
            rows_of = piece_f[k, pl.ds(pl.multiple_of(step * 8, 8), 8)]
            for j in range(8):
                lanes = pl.ds(pl.multiple_of(step * 8 * blk + j * blk, blk), blk)
                acc = acc + integrals[:, lanes].astype(F32) * rows_of[j : j + 1]
            return acc

        acc = lax.fori_loop(0, blk // 8, body, jnp.zeros((count_aux, blk), F32))
        wide = jnp.concatenate([acc, jnp.zeros((blk - count_aux, blk), F32)], axis=0)
        part[pl.ds(k, 1)] = jnp.sum(wide.T, axis=0, keepdims=True)

    top, low = pl.ds(0, blk // 2), pl.ds(blk // 2, blk // 2)
    part[...] = jnp.zeros_like(part)
    piece_of(0)
    whole_x = spread(piece.at[0], got_x.at[0], xs, fx_send.at[0], fx_recv.at[0], over_x)
    piece_x[0] = added(piece.at[0], got_x.at[0], whole_x)
    whole_y = spread(piece_x.at[0], got_y.at[0], ys, fy_send.at[0], fy_recv.at[0], over_y)
    piece_of(1)
    top_x = spread(piece.at[1, top], got_x.at[1, :, top], xs, fx_send.at[1], fx_recv.at[1], over_x)
    low_y = spread(piece.at[1, low], got_y.at[1, :, low], ys, fy_send.at[2], fy_recv.at[2], over_y)
    piece_y[0] = added(piece_x.at[0], got_y.at[0], whole_y)
    whole_c = spread(piece_y.at[0], got_c.at[0], 2, fc_send.at[0], fc_recv.at[0], other_core)
    piece_x[1, top] = added(piece.at[1, top], got_x.at[1, :, top], top_x)
    top_y = spread(piece_x.at[1, top], got_y.at[1, :, top], ys, fy_send.at[1], fy_recv.at[1], over_y)
    piece_x[1, low] = added(piece.at[1, low], got_y.at[1, :, low], low_y)
    low_x = spread(piece_x.at[1, low], got_x.at[1, :, low], xs, fx_send.at[2], fx_recv.at[2], over_x)
    piece_f[0] = added(piece_y.at[0], got_c.at[0], whole_c).astype(F32)
    load_t.wait()
    contract(0)
    piece_y[1, top] = added(piece_x.at[1, top], got_y.at[1, :, top], top_y)
    top_c = spread(piece_y.at[1, top], got_c.at[1, :, top], 2, fc_send.at[1], fc_recv.at[1], other_core)
    piece_y[1, low] = added(piece_x.at[1, low], got_x.at[1, :, low], low_x)
    low_c = spread(piece_y.at[1, low], got_c.at[1, :, low], 2, fc_send.at[2], fc_recv.at[2], other_core)
    piece_f[1, top] = added(piece_y.at[1, top], got_c.at[1, :, top], top_c).astype(F32)
    piece_f[1, low] = added(piece_y.at[1, low], got_c.at[1, :, low], low_c).astype(F32)
    contract(1)

    parts_z[z] = part[...]
    z_copies = [
        remote(part, parts_z.at[z], z_send.at[d - 1], z_recv.at[d - 1], aux, (z + d) % zs)
        for d in range(1, zs)
    ]
    for c in z_copies:
        c.start()
    for c in z_copies:
        c.wait_recv()
    total = parts_z[0]
    for d in range(1, zs):
        total = total + parts_z[d]
    sums[aux] = total

    group = 2 * xs
    e = 2 * x + core
    g_copies = [
        remote(sums.at[aux], sums.at[aux], g_send.at[d - 1], g_recv.at[d - 1], group * y + (e + d) % group, z)
        for d in range(1, group)
    ]
    for c in g_copies:
        c.start()
    for c in g_copies:
        c.wait_recv()
    mine = sums.at[pl.ds(group * y, group)]
    h_copies = [
        remote(mine, mine, h_send.at[d - 1], h_recv.at[d - 1], 2 * (((y + d) % ys) * xs + x) + core, z)
        for d in range(1, ys)
    ]
    for c in h_copies:
        c.start()
    for c in h_copies:
        c.wait_recv()

    load_m.wait()
    lane = lax.broadcasted_iota(jnp.int32, (8, blk), 1)
    acc = [jnp.zeros((count_aux, blk), F32) for _ in range(2)]
    for group_of in range(naux // 4):
        one, two, three, four = (sums[4 * group_of + j] for j in range(4))
        two = pltpu.roll(two, 96, 1)
        three = pltpu.roll(three, 64, 1)
        four = pltpu.roll(four, 32, 1)
        filled = (
            jnp.where(lane < 96, one, two),
            jnp.where(lane < 64, two, three),
            jnp.where(lane < 32, three, four),
        )
        for j, values in enumerate(filled):
            block = metric[:, pl.ds((3 * group_of + j) * blk, blk)]
            for k in range(2):
                acc[k] = acc[k] + block * values[k : k + 1]
    for k in range(2):
        wide = jnp.concatenate([acc[k], jnp.zeros((blk - count_aux, blk), F32)], axis=0)
        coefficients[0, pl.ds(k, 1)] = jnp.sum(wide.T, axis=0, keepdims=True)[:, :count_aux]

    for c in pending + z_copies + g_copies + h_copies:
        c.wait_send()
    for r in range(rows):
        to_aux, to_z = dest_of(r)

        @pl.when(jnp.logical_not((to_aux == aux) & (to_z == z)))
        def _():
            for mat in range(3):
                dst = win1.at[mat, z, pl.ds(own_lo, blk)]
                remote(staged.at[mat, r], dst, in_send.at[mat, r], in_recv.at[mat, z], to_aux, to_z).wait_send()
            remote(keep_src.at[r], keep.at[z], keep_send.at[r], keep_recv.at[z], to_aux, to_z).wait_send()
    for s in range(slots):
        @pl.when(jnp.logical_not((src_aux == aux) & (z == s)))
        def _():
            for k in range(2):
                remote(
                    result.at[k, s], out.at[k, src_row, 0], out_send.at[k, s], out_recv.at[k, src_row], src_aux, s
                ).wait_send()
    for c in range(2):
        @pl.when(core == c)
        def _():
            sends = [one for stage in plan[c] for one in stage[1]]
            for phase, win in enumerate((win1, win2)):
                for mat in range(3):
                    for index, (t, offset) in enumerate(sends):
                        message(win, phase, mat, index, t, offset).wait_send()


def solution(mesh):
    naux, zs = mesh.shape["aux"], mesh.shape["orb"]
    side = {32: (4, 4), 8: (2, 2), 4: (1, 2), 2: (1, 1)}[naux]
    ys, xs = side

    def on_device(band_pattern, density_in, field_terms, fit_blocks, tensor, metric_inv):
        rows = density_in.shape[0]
        slots = zs
        blk = density_in.shape[2]
        count_aux = tensor.shape[1]
        dma = pltpu.SemaphoreType.DMA
        vmem = pltpu.VMEM
        block = (blk, blk)
        in_hbm = pl.BlockSpec(memory_space=pltpu.HBM)
        smem = pl.BlockSpec(memory_space=pltpu.SMEM)
        in_vmem = pl.BlockSpec(memory_space=pltpu.VMEM)
        return pl.pallas_call(
            functools.partial(ring_kernel, (ys, xs, zs, rows, slots)),
            out_shape=(
                jax.ShapeDtypeStruct(field_terms.shape, BF16),
                jax.ShapeDtypeStruct((1, 2, count_aux), F32),
            ),
            in_specs=[smem, smem, in_hbm, in_hbm, in_hbm, in_hbm],
            out_specs=(in_vmem, in_vmem),
            scratch_shapes=[
                vmem((naux, 8, blk), F32),
                vmem((count_aux, naux * count_aux), F32),
                vmem((3, rows, *block), BF16),
                vmem((rows, 8, blk), jnp.int32),
                vmem((slots, 8, blk), jnp.int32),
                vmem((3, slots, slots * blk, blk), BF16),
                vmem((3, slots, slots * blk, blk), BF16),
                vmem((3, blk, slots * blk), BF16),
                vmem((3, blk, slots * blk), BF16),
                vmem((2, slots, *block), BF16),
                vmem((count_aux, blk * blk), BF16),
                vmem((2, *block), BF16),
                vmem((2, *block), BF16),
                vmem((2, *block), BF16),
                vmem((2, max(xs - 1, 1), *block), BF16),
                vmem((2, max(ys - 1, 1), *block), BF16),
                vmem((2, 1, *block), BF16),
                vmem((2, *block), F32),
                vmem((8, blk), F32),
                vmem((zs, 8, blk), F32),
                dma((5,)),
                dma((3, rows)), dma((3, slots)),
                dma((rows,)), dma((slots,)),
                dma((2, 3, slots)), dma((2, 3, slots)),
                dma((2, slots)), dma((2, rows)),
                dma((3, max(xs - 1, 1))), dma((3, max(xs - 1, 1))),
                dma((3, max(ys - 1, 1))), dma((3, max(ys - 1, 1))),
                dma((3, 1)), dma((3, 1)),
                dma((zs,)), dma((zs,)),
                dma((2 * xs,)), dma((2 * xs,)),
                dma((max(ys - 1, 1),)), dma((max(ys - 1, 1),)),
            ],
            compiler_params=pltpu.CompilerParams(
                collective_id=0, has_side_effects=True, vmem_limit_bytes=62 << 20
            ),
        )(
            band_pattern, fit_blocks, density_in, field_terms,
            tensor.reshape(count_aux, blk * blk), metric_inv,
        )

    in_specs = (
        P("aux", None),
        P("aux", "orb", None, None),
        P(None, "aux", "orb", None, None),
        P(),
        P(None, "aux", "orb", None),
        P(None, "aux", None),
    )
    out_specs = (P(None, "aux", "orb", None, None), P(None, None, "aux"))
    return jax.shard_map(
        on_device, mesh=mesh, in_specs=in_specs, out_specs=out_specs, check_vma=False
    )
```

```python
import functools

import jax
import jax.numpy as jnp
from jax import lax
from jax.experimental import pallas as pl
from jax.experimental.pallas import tpu as pltpu
from jax.sharding import PartitionSpec as P

MESH = pl.DeviceIdType.MESH
BF16 = jnp.bfloat16
F32 = jnp.float32


def ring_kernel(
    sizes,
    pattern, fit_blocks, density_hbm, fields_hbm, tensor_hbm, metric_hbm,
    out, coefficients, sums, metric,
    staged, keep_src, keep, win1, win2, lhs1, lhs2, result,
    integrals, piece, piece_x, got_x, got_y, piece_f, part, parts_z,
    load_sem, in_send, in_recv, keep_send, keep_recv,
    win_send, win_recv,
    out_send, out_recv,
    fx_send, fx_recv, fy_send, fy_recv,
    z_send, z_recv, g_send, g_recv, h_send, h_recv,
):
    ys, xs, zs, rows, slots = sizes
    half = slots // 2
    blk = 128
    naux = ys * xs * 2
    total_rows = naux * rows
    aux = lax.axis_index("aux")
    z = lax.axis_index("orb")
    core = aux % 2
    col = aux // 2
    x = col % xs
    y = col // xs
    own_lo = half * blk

    def remote(src, dst, ss, rs, to_aux, to_z):
        return pltpu.make_async_remote_copy(
            src_ref=src, dst_ref=dst, send_sem=ss, recv_sem=rs,
            device_id={"aux": to_aux, "orb": to_z}, device_id_type=MESH,
        )

    def landed(ref, sem):
        pltpu.make_async_copy(ref, ref, sem).wait()

    row = 2 * zs * col + 2 * (z + col % 2 * (zs - 1 - 2 * z)) + core

    def holder(i):
        i = (i + total_rows) % total_rows
        q = (i % (2 * zs)) // 2
        c = i // (2 * zs)
        return 2 * c + i % 2, q + c % 2 * (zs - 1 - 2 * q)

    def dest_of(r):
        return holder(aux * rows + r)

    src_aux, src_row = row // rows, row % rows

    load_d = pltpu.make_async_copy(density_hbm.at[:, 0], staged.at[0], load_sem.at[0])
    load_p = [
        pltpu.make_async_copy(fields_hbm.at[k, :, 0], staged.at[1 + k], load_sem.at[1 + k])
        for k in range(2)
    ]
    load_t = pltpu.make_async_copy(tensor_hbm, integrals, load_sem.at[3])
    load_d.start()
    load_p[0].start()
    load_p[1].start()
    load_t.start()
    load_m = pltpu.make_async_copy(metric_hbm.at[0], metric, load_sem.at[4])
    load_m.start()

    barrier = pltpu.get_barrier_semaphore()
    greeted = 0

    def greet(a, b):
        pl.semaphore_signal(barrier, inc=1, device_id={"aux": a, "orb": b}, device_id_type=MESH)

    for step in range(1, 2 * zs):
        e = (2 * z + core + step) % (2 * zs)
        greet(2 * col + e % 2, e // 2)
    greeted += 2 * zs - 1
    for offset in (-2, -1, 1, 2):
        to_aux, to_z = holder(row + offset)

        @pl.when(to_aux // 2 != col)
        def _():
            greet(to_aux, to_z)

    place = row % (2 * zs)
    near_end = (place < 2) | (place >= 2 * zs - 2)
    at_end = (place < 1) | (place >= 2 * zs - 1)
    for step in range(1, 2 * xs):
        e = (2 * x + core + step) % (2 * xs)

        @pl.when(e // 2 != x)
        def _():
            greet(2 * xs * y + e, z)

    for step in range(1, 2 * ys):
        e = (2 * y + core + step) % (2 * ys)

        @pl.when(e // 2 != y)
        def _():
            greet(2 * (e // 2 * xs + x) + e % 2, z)

    greeted += 2 * (xs - 1) + 2 * (ys - 1)

    first_row = aux * rows
    column = first_row + z - half

    def mask_of(r):
        there = (pattern[r, z] == 1) & (column + r >= 0) & (column + r < total_rows)
        return jnp.where(there, 1, 0)

    for r in range(rows):
        keep_src[r] = jnp.full((8, blk), mask_of(r), jnp.int32)

    load_d.wait()
    for r in range(rows):
        factor = jnp.full((blk, blk), mask_of(r).astype(F32), F32).astype(BF16)
        staged[0, r] = staged[0, r] * factor

    pl.semaphore_wait(barrier, greeted + jnp.where(near_end, 1, 0) + jnp.where(at_end, 1, 0))

    def send_in(mat, r):
        to_aux, to_z = dest_of(r)
        here = (to_aux == aux) & (to_z == z)
        dst = win1.at[mat, z, pl.ds(own_lo, blk)]

        @pl.when(here)
        def _():
            pltpu.make_async_copy(staged.at[mat, r], dst, in_recv.at[mat, z]).start()

        @pl.when(jnp.logical_not(here))
        def _():
            remote(staged.at[mat, r], dst, in_send.at[mat, r], in_recv.at[mat, z], to_aux, to_z).start()

    def send_keep(r):
        to_aux, to_z = dest_of(r)
        here = (to_aux == aux) & (to_z == z)

        @pl.when(here)
        def _():
            pltpu.make_async_copy(keep_src.at[r], keep.at[z], keep_recv.at[z]).start()

        @pl.when(jnp.logical_not(here))
        def _():
            remote(keep_src.at[r], keep.at[z], keep_send.at[r], keep_recv.at[z], to_aux, to_z).start()

    for r in range(rows):
        send_in(0, r)
    for r in range(rows):
        send_keep(r)
    for k in range(2):
        load_p[k].wait()
        for r in range(rows):
            factor = jnp.full((blk, blk), mask_of(r).astype(F32), F32).astype(BF16)
            staged[1 + k, r] = staged[1 + k, r] * factor
        for r in range(rows):
            send_in(1 + k, r)

    for t in range(slots):
        empty = range(t + half, slots) if t < half else range(0, t - half)
        for s in empty:
            for mat in range(3):
                win1[mat, s, pl.ds(t * blk, blk)] = jnp.zeros((blk, blk), BF16)
                win2[mat, s, pl.ds(t * blk, blk)] = jnp.zeros((blk, blk), BF16)

    def slots_of(t):
        return max(0, t - half), min(slots, t + half)

    def message(win, phase, mat, index, t, offset):
        to = t - offset
        lo, hi = slots_of(to)
        to_aux, to_z = holder(row + offset)
        return remote(
            win.at[mat, pl.ds(lo + offset, hi - lo), pl.ds(t * blk, blk)],
            win.at[mat, pl.ds(lo, hi - lo), pl.ds(to * blk, blk)],
            win_send.at[phase, mat, index], win_recv.at[phase, mat, to], to_aux, to_z,
        )

    def got(win, phase, mat, t):
        lo, hi = slots_of(t)
        landed(win.at[mat, pl.ds(lo, hi - lo), pl.ds(t * blk, blk)], win_recv.at[phase, mat, t])

    plan = (
        (
            ((), ((half, 2), (half, -1), (half, 1))),
            ((3, 2), ((3, 2), (2, 2), (3, 1), (2, 1))),
            ((1, 0), ((1, 1),)),
            ((5, 6, 7), ()),
        ),
        (
            ((), ((half, 1), (half, -2), (half, -1))),
            ((5, 6), ((5, -2), (5, -1), (6, -1))),
            ((7,), ()),
            ((3, 2, 1, 0), ()),
        ),
    )

    def advance(win, phase, mat, step):
        for c in range(2):
            @pl.when(core == c)
            def _():
                waits, sends = plan[c][step - 1]
                index = sum(len(plan[c][j][1]) for j in range(step - 1))
                for t in waits:
                    got(win, phase, mat, t)
                for t, offset in sends:
                    message(win, phase, mat, index, t, offset).start()
                    index += 1

    def arrived(mat):
        for u in range(slots):
            landed(win1.at[mat, u, pl.ds(own_lo, blk)], in_recv.at[mat, u])
        for u in range(slots):
            lhs1[mat, :, pl.ds(u * blk, blk)] = win1[mat, u, pl.ds(own_lo, blk)]

    def kept(s, value):
        mask = jnp.broadcast_to(keep[s, pl.ds(0, 1), :], (blk, blk))
        return jnp.where(mask > 0, value, 0.0)

    def square():
        def body(s, carry):
            value = jnp.dot(lhs1[0], win1[0, s], preferred_element_type=F32)
            win2[0, s, pl.ds(own_lo, blk)] = kept(s, value).astype(BF16)
            return carry

        lax.fori_loop(0, slots, body, 0)
        for s in range(slots):
            lhs2[0, :, pl.ds(s * blk, blk)] = win2[0, s, pl.ds(own_lo, blk)]

    def first(k):
        def body(s, carry):
            value = jnp.dot(lhs1[0], win1[1 + k, s], preferred_element_type=F32)
            value = value + jnp.dot(lhs1[1 + k], win1[0, s], preferred_element_type=F32)
            win2[1 + k, s, pl.ds(own_lo, blk)] = kept(s, value).astype(BF16)
            return carry

        lax.fori_loop(0, slots, body, 0)
        for s in range(slots):
            lhs2[1 + k, :, pl.ds(s * blk, blk)] = win2[1 + k, s, pl.ds(own_lo, blk)]

    def send_out(k, s):
        here = (src_aux == aux) & (z == s)
        dst = out.at[k, src_row, 0]

        @pl.when(here)
        def _():
            pltpu.make_async_copy(result.at[k, s], dst, out_recv.at[k, src_row]).start()

        @pl.when(jnp.logical_not(here))
        def _():
            remote(result.at[k, s], dst, out_send.at[k, s], out_recv.at[k, src_row], src_aux, s).start()

    def second(k):
        def body(s, carry):
            value = jnp.dot(lhs2[0], win2[1 + k, s], preferred_element_type=F32)
            value = value + jnp.dot(lhs2[1 + k], win2[0, s], preferred_element_type=F32)
            value = 2.0 * win2[1 + k, s, pl.ds(own_lo, blk)].astype(F32) - value
            result[k, s] = kept(s, value).astype(BF16)
            send_out(k, s)
            return carry

        lax.fori_loop(0, slots, body, 0)

    done = 4
    order = (
        "D1", "P1", "D2", "S1", "P2", "D3", "D4", "Q1",
        "S2", "P3", "P4", "F1", "Q2", "S3", "S4", "G1",
        "F2", "Q3", "G2", "F3", "Q4", "F4", "G3", "G4",
    )
    item_of = {"D": 0, "P": 1, "S": 2, "Q": 3, "F": 4, "G": 5}
    for word in order:
        item, step = item_of[word[0]], int(word[1])
        phase, mat = item // 3, item % 3
        if step == 1 and phase == 0:
            arrived(mat)
        if step == 1 and phase == 1:
            if mat == 0:
                for u in range(slots):
                    landed(keep.at[u], keep_recv.at[u])
                square()
            else:
                first(mat - 1)
        advance(win1 if phase == 0 else win2, phase, mat, step)
        if step == done and phase == 1 and mat > 0:
            second(mat - 1)

    fitted = fit_blocks[0]

    def over_x(d):
        return 2 * (y * xs + (x + d) % xs) + core

    def over_y(d):
        return 2 * (((y + d) % ys) * xs + x) + core

    pending = []

    def spread(src, got_there, count, ss, rs, target):
        copies = [
            remote(src, got_there.at[d - 1], ss.at[d - 1], rs.at[d - 1], target(d), z)
            for d in range(1, count)
        ]
        for c in copies:
            c.start()
        pending.extend(copies)
        return copies

    def added(src, got_there, copies):
        value = src[...]
        for d, c in enumerate(copies):
            c.wait_recv()
            value = value + got_there[d]
        return value

    def piece_of(k):
        for r in range(rows):
            landed(out.at[k, r, 0], out_recv.at[k, r])
        value = jnp.zeros((blk, blk), BF16)
        for r in range(rows):
            chosen = jnp.where(fitted == first_row + r, 1.0, 0.0)
            value = value + out[k, r, 0] * jnp.full((blk, blk), chosen, F32).astype(BF16)
        piece[k] = value

    count_aux = integrals.shape[0]

    def contract(k):
        def body(step, acc):
            rows_of = piece_f[k, pl.ds(pl.multiple_of(step * 8, 8), 8)]
            for j in range(8):
                lanes = pl.ds(pl.multiple_of(step * 8 * blk + j * blk, blk), blk)
                acc = acc + integrals[:, lanes].astype(F32) * rows_of[j : j + 1]
            return acc

        acc = lax.fori_loop(0, blk // 8, body, jnp.zeros((count_aux, blk), F32))
        wide = jnp.concatenate([acc, jnp.zeros((blk - count_aux, blk), F32)], axis=0)
        part[pl.ds(k, 1)] = jnp.sum(wide.T, axis=0, keepdims=True)

    def x_cores(d):
        return 2 * xs * y + (2 * x + core + d) % (2 * xs)

    def y_cores(d):
        e = (2 * y + core + d) % (2 * ys)
        return 2 * (e // 2 * xs + x) + e % 2

    top, low = pl.ds(0, blk // 2), pl.ds(blk // 2, blk // 2)
    piece_of(0)
    whole_1 = spread(piece.at[0], got_x.at[0], 2 * xs, fx_send.at[0], fx_recv.at[0], x_cores)
    piece_x[0] = added(piece.at[0], got_x.at[0], whole_1)
    whole_2 = spread(piece_x.at[0], got_y.at[0], ys, fy_send.at[0], fy_recv.at[0], over_y)
    piece_of(1)
    top_1 = spread(piece.at[1, top], got_x.at[1, :, top], 2 * xs, fx_send.at[1], fx_recv.at[1], x_cores)
    low_1 = spread(piece.at[1, low], got_x.at[1, :, low], 2 * ys, fx_send.at[2], fx_recv.at[2], y_cores)
    piece_f[0] = added(piece_x.at[0], got_y.at[0], whole_2).astype(F32)
    piece_x[1, top] = added(piece.at[1, top], got_x.at[1, :, top], top_1)
    top_2 = spread(piece_x.at[1, top], got_y.at[1, :, top], ys, fy_send.at[1], fy_recv.at[1], over_y)
    piece_x[1, low] = added(piece.at[1, low], got_x.at[1, :, low], low_1)
    low_2 = spread(piece_x.at[1, low], got_y.at[1, :, low], xs, fy_send.at[2], fy_recv.at[2], over_x)
    load_t.wait()
    contract(0)
    piece_f[1, top] = added(piece_x.at[1, top], got_y.at[1, :, top], top_2).astype(F32)
    piece_f[1, low] = added(piece_x.at[1, low], got_y.at[1, :, low], low_2).astype(F32)
    contract(1)

    parts_z[z] = part[...]
    z_copies = [
        remote(part, parts_z.at[z], z_send.at[d - 1], z_recv.at[d - 1], aux, (z + d) % zs)
        for d in range(1, zs)
    ]
    for c in z_copies:
        c.start()
    for c in z_copies:
        c.wait_recv()
    total = parts_z[0]
    for d in range(1, zs):
        total = total + parts_z[d]
    sums[aux] = total

    group = 2 * xs
    e = 2 * x + core
    g_copies = [
        remote(sums.at[aux], sums.at[aux], g_send.at[d - 1], g_recv.at[d - 1], group * y + (e + d) % group, z)
        for d in range(1, group)
    ]
    for c in g_copies:
        c.start()
    for c in g_copies:
        c.wait_recv()
    mine = sums.at[pl.ds(group * y, group)]
    h_copies = [
        remote(mine, mine, h_send.at[d - 1], h_recv.at[d - 1], 2 * (((y + d) % ys) * xs + x) + core, z)
        for d in range(1, ys)
    ]
    for c in h_copies:
        c.start()
    for c in h_copies:
        c.wait_recv()

    load_m.wait()
    lane = lax.broadcasted_iota(jnp.int32, (1, blk), 1)
    acc = [jnp.zeros((count_aux, blk), F32) for _ in range(2)]
    for group_of in range(naux // 4):
        pieces = jnp.concatenate([sums[4 * group_of + j] for j in range(4)], axis=0)
        by96, by64, by32 = (pltpu.roll(pieces, shift, 1) for shift in (96, 64, 32))
        for k in range(2):
            one = pieces[k : k + 1]
            two = by96[2 + k : 3 + k]
            three = by64[4 + k : 5 + k]
            four = by32[6 + k : 7 + k]
            filled = (
                jnp.where(lane < 96, one, two),
                jnp.where(lane < 64, two, three),
                jnp.where(lane < 32, three, four),
            )
            for j, values in enumerate(filled):
                acc[k] = acc[k] + metric[:, pl.ds((3 * group_of + j) * blk, blk)] * values
    for k in range(2):
        wide = jnp.concatenate([acc[k], jnp.zeros((blk - count_aux, blk), F32)], axis=0)
        coefficients[0, pl.ds(k, 1)] = jnp.sum(wide.T, axis=0, keepdims=True)[:, :count_aux]

    for c in pending + z_copies + g_copies + h_copies:
        c.wait_send()
    for r in range(rows):
        to_aux, to_z = dest_of(r)

        @pl.when(jnp.logical_not((to_aux == aux) & (to_z == z)))
        def _():
            for mat in range(3):
                dst = win1.at[mat, z, pl.ds(own_lo, blk)]
                remote(staged.at[mat, r], dst, in_send.at[mat, r], in_recv.at[mat, z], to_aux, to_z).wait_send()
            remote(keep_src.at[r], keep.at[z], keep_send.at[r], keep_recv.at[z], to_aux, to_z).wait_send()
    for s in range(slots):
        @pl.when(jnp.logical_not((src_aux == aux) & (z == s)))
        def _():
            for k in range(2):
                remote(
                    result.at[k, s], out.at[k, src_row, 0], out_send.at[k, s], out_recv.at[k, src_row], src_aux, s
                ).wait_send()
    for c in range(2):
        @pl.when(core == c)
        def _():
            sends = [one for stage in plan[c] for one in stage[1]]
            for phase, win in enumerate((win1, win2)):
                for mat in range(3):
                    for index, (t, offset) in enumerate(sends):
                        message(win, phase, mat, index, t, offset).wait_send()


def solution(mesh):
    naux, zs = mesh.shape["aux"], mesh.shape["orb"]
    side = {32: (4, 4), 8: (2, 2), 4: (1, 2), 2: (1, 1)}[naux]
    ys, xs = side

    def on_device(band_pattern, density_in, field_terms, fit_blocks, tensor, metric_inv):
        rows = density_in.shape[0]
        slots = zs
        blk = density_in.shape[2]
        count_aux = tensor.shape[1]
        dma = pltpu.SemaphoreType.DMA
        vmem = pltpu.VMEM
        block = (blk, blk)
        in_hbm = pl.BlockSpec(memory_space=pltpu.HBM)
        smem = pl.BlockSpec(memory_space=pltpu.SMEM)
        in_vmem = pl.BlockSpec(memory_space=pltpu.VMEM)
        return pl.pallas_call(
            functools.partial(ring_kernel, (ys, xs, zs, rows, slots)),
            out_shape=(
                jax.ShapeDtypeStruct(field_terms.shape, BF16),
                jax.ShapeDtypeStruct((1, 2, count_aux), F32),
            ),
            in_specs=[smem, smem, in_hbm, in_hbm, in_hbm, in_hbm],
            out_specs=(in_vmem, in_vmem),
            scratch_shapes=[
                vmem((naux, 2, blk), F32),
                vmem((count_aux, naux * count_aux), F32),
                vmem((3, rows, *block), BF16),
                vmem((rows, 8, blk), jnp.int32),
                vmem((slots, 8, blk), jnp.int32),
                vmem((3, slots, slots * blk, blk), BF16),
                vmem((3, slots, slots * blk, blk), BF16),
                vmem((3, blk, slots * blk), BF16),
                vmem((3, blk, slots * blk), BF16),
                vmem((2, slots, *block), BF16),
                vmem((count_aux, blk * blk), BF16),
                vmem((2, *block), BF16),
                vmem((2, *block), BF16),
                vmem((2, 2 * max(xs, ys) - 1, *block), BF16),
                vmem((2, max(xs, ys) - 1, *block), BF16),
                vmem((2, *block), F32),
                vmem((2, blk), F32),
                vmem((zs, 2, blk), F32),
                dma((5,)),
                dma((3, rows)), dma((3, slots)),
                dma((rows,)), dma((slots,)),
                dma((2, 3, slots)), dma((2, 3, slots)),
                dma((2, slots)), dma((2, rows)),
                dma((3, 2 * max(xs, ys) - 1)), dma((3, 2 * max(xs, ys) - 1)),
                dma((3, max(xs, ys) - 1)), dma((3, max(xs, ys) - 1)),
                dma((zs,)), dma((zs,)),
                dma((2 * xs,)), dma((2 * xs,)),
                dma((max(ys - 1, 1),)), dma((max(ys - 1, 1),)),
            ],
            compiler_params=pltpu.CompilerParams(
                collective_id=0, has_side_effects=True, vmem_limit_bytes=62 << 20
            ),
        )(
            band_pattern, fit_blocks, density_in, field_terms,
            tensor.reshape(count_aux, blk * blk), metric_inv,
        )

    in_specs = (
        P("aux", None),
        P("aux", "orb", None, None),
        P(None, "aux", "orb", None, None),
        P(),
        P(None, "aux", "orb", None),
        P(None, "aux", None),
    )
    out_specs = (P(None, "aux", "orb", None, None), P(None, None, "aux"))
    return jax.shard_map(
        on_device, mesh=mesh, in_specs=in_specs, out_specs=out_specs, check_vma=False
    )
```

```python
import functools

import jax
import jax.numpy as jnp
from jax import lax
from jax.experimental import pallas as pl
from jax.experimental.pallas import tpu as pltpu
from jax.sharding import PartitionSpec as P

MESH = pl.DeviceIdType.MESH
BF16 = jnp.bfloat16
F32 = jnp.float32


def ring_kernel(
    sizes,
    pattern, fit_blocks, density_hbm, fields_hbm, tensor_hbm, metric_hbm,
    out, coefficients, sums, metric,
    staged, keep_src, keep, win1, win2, lhs1, lhs2, result,
    integrals, piece, piece_x, got_x, got_y, piece_f, part, parts_z,
    load_sem, in_send, in_recv, keep_send, keep_recv,
    win_send, win_recv,
    out_send, out_recv,
    fx_send, fx_recv, fy_send, fy_recv,
    z_send, z_recv, g_send, g_recv,
):
    ys, xs, zs, rows, slots = sizes
    half = slots // 2
    blk = 128
    naux = ys * xs * 2
    total_rows = naux * rows
    aux = lax.axis_index("aux")
    z = lax.axis_index("orb")
    core = aux % 2
    col = aux // 2
    x = col % xs
    y = col // xs
    own_lo = half * blk

    def remote(src, dst, ss, rs, to_aux, to_z):
        return pltpu.make_async_remote_copy(
            src_ref=src, dst_ref=dst, send_sem=ss, recv_sem=rs,
            device_id={"aux": to_aux, "orb": to_z}, device_id_type=MESH,
        )

    def landed(ref, sem):
        pltpu.make_async_copy(ref, ref, sem).wait()

    row = 2 * zs * col + 2 * (z + col % 2 * (zs - 1 - 2 * z)) + core

    def holder(i):
        i = (i + total_rows) % total_rows
        q = (i % (2 * zs)) // 2
        c = i // (2 * zs)
        return 2 * c + i % 2, q + c % 2 * (zs - 1 - 2 * q)

    def dest_of(r):
        return holder(aux * rows + r)

    src_aux, src_row = row // rows, row % rows

    load_d = pltpu.make_async_copy(density_hbm.at[:, 0], staged.at[0], load_sem.at[0])
    load_p = [
        pltpu.make_async_copy(fields_hbm.at[k, :, 0], staged.at[1 + k], load_sem.at[1 + k])
        for k in range(2)
    ]
    load_t = pltpu.make_async_copy(tensor_hbm, integrals, load_sem.at[3])
    load_d.start()
    load_p[0].start()
    load_p[1].start()
    load_t.start()
    load_m = pltpu.make_async_copy(metric_hbm.at[0], metric, load_sem.at[4])
    load_m.start()

    barrier = pltpu.get_barrier_semaphore()
    greeted = 0

    def greet(a, b):
        pl.semaphore_signal(barrier, inc=1, device_id={"aux": a, "orb": b}, device_id_type=MESH)

    for step in range(1, 2 * zs):
        e = (2 * z + core + step) % (2 * zs)
        greet(2 * col + e % 2, e // 2)
    greeted += 2 * zs - 1
    for offset in (-2, -1, 1, 2):
        to_aux, to_z = holder(row + offset)

        @pl.when(to_aux // 2 != col)
        def _():
            greet(to_aux, to_z)

    place = row % (2 * zs)
    near_end = (place < 2) | (place >= 2 * zs - 2)
    at_end = (place < 1) | (place >= 2 * zs - 1)
    for step in range(1, 2 * xs):
        e = (2 * x + core + step) % (2 * xs)

        @pl.when(e // 2 != x)
        def _():
            greet(2 * xs * y + e, z)

    for step in range(1, 2 * ys):
        e = (2 * y + core + step) % (2 * ys)

        @pl.when(e // 2 != y)
        def _():
            greet(2 * (e // 2 * xs + x) + e % 2, z)

    for step in range(1, xs * ys):
        c = (col + step) % (xs * ys)

        @pl.when((c % xs != x) & (c // xs != y))
        def _():
            greet(2 * c + core, z)

    greeted += 2 * (xs - 1) + 2 * (ys - 1) + (xs - 1) * (ys - 1)

    first_row = aux * rows
    column = first_row + z - half

    def mask_of(r):
        there = (pattern[r, z] == 1) & (column + r >= 0) & (column + r < total_rows)
        return jnp.where(there, 1, 0)

    for r in range(rows):
        keep_src[r] = jnp.full((8, blk), mask_of(r), jnp.int32)

    load_d.wait()
    for r in range(rows):
        factor = jnp.full((blk, blk), mask_of(r).astype(F32), F32).astype(BF16)
        staged[0, r] = staged[0, r] * factor

    pl.semaphore_wait(barrier, greeted + jnp.where(near_end, 1, 0) + jnp.where(at_end, 1, 0))

    def send_in(mat, r):
        to_aux, to_z = dest_of(r)
        here = (to_aux == aux) & (to_z == z)
        dst = win1.at[mat, z, pl.ds(own_lo, blk)]

        @pl.when(here)
        def _():
            pltpu.make_async_copy(staged.at[mat, r], dst, in_recv.at[mat, z]).start()

        @pl.when(jnp.logical_not(here))
        def _():
            remote(staged.at[mat, r], dst, in_send.at[mat, r], in_recv.at[mat, z], to_aux, to_z).start()

    def send_keep(r):
        to_aux, to_z = dest_of(r)
        here = (to_aux == aux) & (to_z == z)

        @pl.when(here)
        def _():
            pltpu.make_async_copy(keep_src.at[r], keep.at[z], keep_recv.at[z]).start()

        @pl.when(jnp.logical_not(here))
        def _():
            remote(keep_src.at[r], keep.at[z], keep_send.at[r], keep_recv.at[z], to_aux, to_z).start()

    for r in range(rows):
        send_in(0, r)
    for r in range(rows):
        send_keep(r)
    for k in range(2):
        load_p[k].wait()
        for r in range(rows):
            factor = jnp.full((blk, blk), mask_of(r).astype(F32), F32).astype(BF16)
            staged[1 + k, r] = staged[1 + k, r] * factor
        for r in range(rows):
            send_in(1 + k, r)

    for t in range(slots):
        empty = range(t + half, slots) if t < half else range(0, t - half)
        for s in empty:
            for mat in range(3):
                win1[mat, s, pl.ds(t * blk, blk)] = jnp.zeros((blk, blk), BF16)
                win2[mat, s, pl.ds(t * blk, blk)] = jnp.zeros((blk, blk), BF16)

    def slots_of(t):
        return max(0, t - half), min(slots, t + half)

    def message(win, phase, mat, index, t, offset):
        to = t - offset
        lo, hi = slots_of(to)
        to_aux, to_z = holder(row + offset)
        return remote(
            win.at[mat, pl.ds(lo + offset, hi - lo), pl.ds(t * blk, blk)],
            win.at[mat, pl.ds(lo, hi - lo), pl.ds(to * blk, blk)],
            win_send.at[phase, mat, index], win_recv.at[phase, mat, to], to_aux, to_z,
        )

    def got(win, phase, mat, t):
        lo, hi = slots_of(t)
        landed(win.at[mat, pl.ds(lo, hi - lo), pl.ds(t * blk, blk)], win_recv.at[phase, mat, t])

    plan = (
        (
            ((), ((half, 2), (half, -1), (half, 1))),
            ((3, 2), ((3, 2), (2, 2), (3, 1), (2, 1))),
            ((1, 0), ((1, 1),)),
            ((5, 6, 7), ()),
        ),
        (
            ((), ((half, 1), (half, -2), (half, -1))),
            ((5, 6), ((5, -2), (5, -1), (6, -1))),
            ((7,), ()),
            ((3, 2, 1, 0), ()),
        ),
    )

    def advance(win, phase, mat, step):
        for c in range(2):
            @pl.when(core == c)
            def _():
                waits, sends = plan[c][step - 1]
                index = sum(len(plan[c][j][1]) for j in range(step - 1))
                for t in waits:
                    got(win, phase, mat, t)
                for t, offset in sends:
                    message(win, phase, mat, index, t, offset).start()
                    index += 1

    def arrived(mat):
        for u in range(slots):
            landed(win1.at[mat, u, pl.ds(own_lo, blk)], in_recv.at[mat, u])
        for u in range(slots):
            lhs1[mat, :, pl.ds(u * blk, blk)] = win1[mat, u, pl.ds(own_lo, blk)]

    def kept(s, value):
        mask = jnp.broadcast_to(keep[s, pl.ds(0, 1), :], (blk, blk))
        return jnp.where(mask > 0, value, 0.0)

    def square():
        def body(s, carry):
            value = jnp.dot(lhs1[0], win1[0, s], preferred_element_type=F32)
            win2[0, s, pl.ds(own_lo, blk)] = kept(s, value).astype(BF16)
            return carry

        lax.fori_loop(0, slots, body, 0)
        for s in range(slots):
            lhs2[0, :, pl.ds(s * blk, blk)] = win2[0, s, pl.ds(own_lo, blk)]

    def first(k):
        def body(s, carry):
            value = jnp.dot(lhs1[0], win1[1 + k, s], preferred_element_type=F32)
            value = value + jnp.dot(lhs1[1 + k], win1[0, s], preferred_element_type=F32)
            win2[1 + k, s, pl.ds(own_lo, blk)] = kept(s, value).astype(BF16)
            return carry

        lax.fori_loop(0, slots, body, 0)
        for s in range(slots):
            lhs2[1 + k, :, pl.ds(s * blk, blk)] = win2[1 + k, s, pl.ds(own_lo, blk)]

    def send_out(k, s):
        here = (src_aux == aux) & (z == s)
        dst = out.at[k, src_row, 0]

        @pl.when(here)
        def _():
            pltpu.make_async_copy(result.at[k, s], dst, out_recv.at[k, src_row]).start()

        @pl.when(jnp.logical_not(here))
        def _():
            remote(result.at[k, s], dst, out_send.at[k, s], out_recv.at[k, src_row], src_aux, s).start()

    def second(k):
        def body(s, carry):
            value = jnp.dot(lhs2[0], win2[1 + k, s], preferred_element_type=F32)
            value = value + jnp.dot(lhs2[1 + k], win2[0, s], preferred_element_type=F32)
            value = 2.0 * win2[1 + k, s, pl.ds(own_lo, blk)].astype(F32) - value
            result[k, s] = kept(s, value).astype(BF16)
            send_out(k, s)
            return carry

        lax.fori_loop(0, slots, body, 0)

    done = 4
    order = (
        "D1", "P1", "D2", "S1", "P2", "D3", "D4", "Q1",
        "S2", "P3", "P4", "F1", "Q2", "S3", "S4", "G1",
        "F2", "Q3", "G2", "F3", "Q4", "F4", "G3", "G4",
    )
    item_of = {"D": 0, "P": 1, "S": 2, "Q": 3, "F": 4, "G": 5}
    for word in order:
        item, step = item_of[word[0]], int(word[1])
        phase, mat = item // 3, item % 3
        if step == 1 and phase == 0:
            arrived(mat)
        if step == 1 and phase == 1:
            if mat == 0:
                for u in range(slots):
                    landed(keep.at[u], keep_recv.at[u])
                square()
            else:
                first(mat - 1)
        advance(win1 if phase == 0 else win2, phase, mat, step)
        if step == done and phase == 1 and mat > 0:
            second(mat - 1)

    fitted = fit_blocks[0]

    def over_x(d):
        return 2 * (y * xs + (x + d) % xs) + core

    def over_y(d):
        return 2 * (((y + d) % ys) * xs + x) + core

    pending = []

    def spread(src, got_there, count, ss, rs, target):
        copies = [
            remote(src, got_there.at[d - 1], ss.at[d - 1], rs.at[d - 1], target(d), z)
            for d in range(1, count)
        ]
        for c in copies:
            c.start()
        pending.extend(copies)
        return copies

    def added(src, got_there, copies):
        value = src[...]
        for d, c in enumerate(copies):
            c.wait_recv()
            value = value + got_there[d]
        return value

    def piece_of(k):
        for r in range(rows):
            landed(out.at[k, r, 0], out_recv.at[k, r])
        value = jnp.zeros((blk, blk), BF16)
        for r in range(rows):
            chosen = jnp.where(fitted == first_row + r, 1.0, 0.0)
            value = value + out[k, r, 0] * jnp.full((blk, blk), chosen, F32).astype(BF16)
        piece[k] = value

    count_aux = integrals.shape[0]

    def contract(k):
        def body(step, acc):
            rows_of = piece_f[k, pl.ds(pl.multiple_of(step * 8, 8), 8)]
            for j in range(8):
                lanes = pl.ds(pl.multiple_of(step * 8 * blk + j * blk, blk), blk)
                acc = acc + integrals[:, lanes].astype(F32) * rows_of[j : j + 1]
            return acc

        acc = lax.fori_loop(0, blk // 8, body, jnp.zeros((count_aux, blk), F32))
        wide = jnp.concatenate([acc, jnp.zeros((blk - count_aux, blk), F32)], axis=0)
        part[pl.ds(k, 1)] = jnp.sum(wide.T, axis=0, keepdims=True)

    def x_cores(d):
        return 2 * xs * y + (2 * x + core + d) % (2 * xs)

    def y_cores(d):
        e = (2 * y + core + d) % (2 * ys)
        return 2 * (e // 2 * xs + x) + e % 2

    top, low = pl.ds(0, blk // 2), pl.ds(blk // 2, blk // 2)
    piece_of(0)
    whole_1 = spread(piece.at[0], got_x.at[0], 2 * xs, fx_send.at[0], fx_recv.at[0], x_cores)
    piece_x[0] = added(piece.at[0], got_x.at[0], whole_1)
    whole_2 = spread(piece_x.at[0], got_y.at[0], ys, fy_send.at[0], fy_recv.at[0], over_y)
    piece_of(1)
    top_1 = spread(piece.at[1, top], got_x.at[1, :, top], 2 * xs, fx_send.at[1], fx_recv.at[1], x_cores)
    low_1 = spread(piece.at[1, low], got_x.at[1, :, low], 2 * ys, fx_send.at[2], fx_recv.at[2], y_cores)
    piece_f[0] = added(piece_x.at[0], got_y.at[0], whole_2).astype(F32)
    piece_x[1, top] = added(piece.at[1, top], got_x.at[1, :, top], top_1)
    top_2 = spread(piece_x.at[1, top], got_y.at[1, :, top], ys, fy_send.at[1], fy_recv.at[1], over_y)
    piece_x[1, low] = added(piece.at[1, low], got_x.at[1, :, low], low_1)
    low_2 = spread(piece_x.at[1, low], got_y.at[1, :, low], xs, fy_send.at[2], fy_recv.at[2], over_x)
    load_t.wait()
    contract(0)
    piece_f[1, top] = added(piece_x.at[1, top], got_y.at[1, :, top], top_2).astype(F32)
    piece_f[1, low] = added(piece_x.at[1, low], got_y.at[1, :, low], low_2).astype(F32)
    contract(1)

    e = 2 * z + core
    parts_z[e] = part[...]
    z_copies = []
    for d in range(1, 2 * zs):
        f = (e + d) % (2 * zs)
        z_copies.append(remote(part, parts_z.at[e], z_send.at[d - 1], z_recv.at[d - 1], 2 * col + f % 2, f // 2))
    for c in z_copies:
        c.start()
    for c in z_copies:
        c.wait_recv()
    for c in range(2):
        total = parts_z[c]
        for d in range(1, zs):
            total = total + parts_z[2 * d + c]
        sums[2 * col + c] = total
    mine = sums.at[pl.ds(2 * col, 2)]
    g_copies = [
        remote(mine, mine, g_send.at[d - 1], g_recv.at[d - 1], 2 * ((col + d) % (xs * ys)) + core, z)
        for d in range(1, xs * ys)
    ]
    for c in g_copies:
        c.start()
    for c in g_copies:
        c.wait_recv()

    load_m.wait()
    lane = lax.broadcasted_iota(jnp.int32, (1, blk), 1)
    acc = [jnp.zeros((count_aux, blk), F32) for _ in range(2)]
    for group_of in range(naux // 4):
        pieces = jnp.concatenate([sums[4 * group_of + j] for j in range(4)], axis=0)
        by96, by64, by32 = (pltpu.roll(pieces, shift, 1) for shift in (96, 64, 32))
        for k in range(2):
            one = pieces[k : k + 1]
            two = by96[2 + k : 3 + k]
            three = by64[4 + k : 5 + k]
            four = by32[6 + k : 7 + k]
            filled = (
                jnp.where(lane < 96, one, two),
                jnp.where(lane < 64, two, three),
                jnp.where(lane < 32, three, four),
            )
            for j, values in enumerate(filled):
                acc[k] = acc[k] + metric[:, pl.ds((3 * group_of + j) * blk, blk)] * values
    for k in range(2):
        wide = jnp.concatenate([acc[k], jnp.zeros((blk - count_aux, blk), F32)], axis=0)
        coefficients[0, pl.ds(k, 1)] = jnp.sum(wide.T, axis=0, keepdims=True)[:, :count_aux]

    for c in pending + z_copies + g_copies:
        c.wait_send()
    for r in range(rows):
        to_aux, to_z = dest_of(r)

        @pl.when(jnp.logical_not((to_aux == aux) & (to_z == z)))
        def _():
            for mat in range(3):
                dst = win1.at[mat, z, pl.ds(own_lo, blk)]
                remote(staged.at[mat, r], dst, in_send.at[mat, r], in_recv.at[mat, z], to_aux, to_z).wait_send()
            remote(keep_src.at[r], keep.at[z], keep_send.at[r], keep_recv.at[z], to_aux, to_z).wait_send()
    for s in range(slots):
        @pl.when(jnp.logical_not((src_aux == aux) & (z == s)))
        def _():
            for k in range(2):
                remote(
                    result.at[k, s], out.at[k, src_row, 0], out_send.at[k, s], out_recv.at[k, src_row], src_aux, s
                ).wait_send()
    for c in range(2):
        @pl.when(core == c)
        def _():
            sends = [one for stage in plan[c] for one in stage[1]]
            for phase, win in enumerate((win1, win2)):
                for mat in range(3):
                    for index, (t, offset) in enumerate(sends):
                        message(win, phase, mat, index, t, offset).wait_send()


def solution(mesh):
    naux, zs = mesh.shape["aux"], mesh.shape["orb"]
    side = {32: (4, 4), 8: (2, 2), 4: (1, 2), 2: (1, 1)}[naux]
    ys, xs = side

    def on_device(band_pattern, density_in, field_terms, fit_blocks, tensor, metric_inv):
        rows = density_in.shape[0]
        slots = zs
        blk = density_in.shape[2]
        count_aux = tensor.shape[1]
        dma = pltpu.SemaphoreType.DMA
        vmem = pltpu.VMEM
        block = (blk, blk)
        in_hbm = pl.BlockSpec(memory_space=pltpu.HBM)
        smem = pl.BlockSpec(memory_space=pltpu.SMEM)
        in_vmem = pl.BlockSpec(memory_space=pltpu.VMEM)
        return pl.pallas_call(
            functools.partial(ring_kernel, (ys, xs, zs, rows, slots)),
            out_shape=(
                jax.ShapeDtypeStruct(field_terms.shape, BF16),
                jax.ShapeDtypeStruct((1, 2, count_aux), F32),
            ),
            in_specs=[smem, smem, in_hbm, in_hbm, in_hbm, in_hbm],
            out_specs=(in_vmem, in_vmem),
            scratch_shapes=[
                vmem((naux, 2, blk), F32),
                vmem((count_aux, naux * count_aux), F32),
                vmem((3, rows, *block), BF16),
                vmem((rows, 8, blk), jnp.int32),
                vmem((slots, 8, blk), jnp.int32),
                vmem((3, slots, slots * blk, blk), BF16),
                vmem((3, slots, slots * blk, blk), BF16),
                vmem((3, blk, slots * blk), BF16),
                vmem((3, blk, slots * blk), BF16),
                vmem((2, slots, *block), BF16),
                vmem((count_aux, blk * blk), BF16),
                vmem((2, *block), BF16),
                vmem((2, *block), BF16),
                vmem((2, 2 * max(xs, ys) - 1, *block), BF16),
                vmem((2, max(xs, ys) - 1, *block), BF16),
                vmem((2, *block), F32),
                vmem((2, blk), F32),
                vmem((2 * zs, 2, blk), F32),
                dma((5,)),
                dma((3, rows)), dma((3, slots)),
                dma((rows,)), dma((slots,)),
                dma((2, 3, slots)), dma((2, 3, slots)),
                dma((2, slots)), dma((2, rows)),
                dma((3, 2 * max(xs, ys) - 1)), dma((3, 2 * max(xs, ys) - 1)),
                dma((3, max(xs, ys) - 1)), dma((3, max(xs, ys) - 1)),
                dma((2 * zs,)), dma((2 * zs,)),
                dma((xs * ys,)), dma((xs * ys,)),
            ],
            compiler_params=pltpu.CompilerParams(
                collective_id=0, has_side_effects=True, vmem_limit_bytes=53 << 20
            ),
        )(
            band_pattern, fit_blocks, density_in, field_terms,
            tensor.reshape(count_aux, blk * blk), metric_inv,
        )

    in_specs = (
        P("aux", None),
        P("aux", "orb", None, None),
        P(None, "aux", "orb", None, None),
        P(),
        P(None, "aux", "orb", None),
        P(None, "aux", None),
    )
    out_specs = (P(None, "aux", "orb", None, None), P(None, None, "aux"))
    return jax.shard_map(
        on_device, mesh=mesh, in_specs=in_specs, out_specs=out_specs, check_vma=False
    )
```

```python
import functools

import jax
import jax.numpy as jnp
from jax import lax
from jax.experimental import pallas as pl
from jax.experimental.pallas import tpu as pltpu
from jax.sharding import PartitionSpec as P

MESH = pl.DeviceIdType.MESH
BF16 = jnp.bfloat16
F32 = jnp.float32


def ring_kernel(
    sizes,
    pattern, fit_blocks, density_hbm, fields_hbm, tensor_hbm, metric_hbm,
    out, coefficients, sums, metric,
    staged, keep_src, keep, win1, win2, lhs1, lhs2, result,
    integrals, piece, piece_x, got_x, got_y, piece_f, part, parts_z,
    load_sem, in_send, in_recv, keep_send, keep_recv,
    win_send, win_recv,
    out_send, out_recv,
    fx_send, fx_recv, fy_send, fy_recv,
    z_send, z_recv, g_send, g_recv,
):
    ys, xs, zs, rows, slots = sizes
    half = slots // 2
    blk = 128
    naux = ys * xs * 2
    total_rows = naux * rows
    aux = lax.axis_index("aux")
    z = lax.axis_index("orb")
    core = aux % 2
    col = aux // 2
    x = col % xs
    y = col // xs
    own_lo = half * blk

    def remote(src, dst, ss, rs, to_aux, to_z):
        return pltpu.make_async_remote_copy(
            src_ref=src, dst_ref=dst, send_sem=ss, recv_sem=rs,
            device_id={"aux": to_aux, "orb": to_z}, device_id_type=MESH,
        )

    def landed(ref, sem):
        pltpu.make_async_copy(ref, ref, sem).wait()

    row = 2 * zs * col + 2 * (z + col % 2 * (zs - 1 - 2 * z)) + core

    def holder(i):
        i = (i + total_rows) % total_rows
        q = (i % (2 * zs)) // 2
        c = i // (2 * zs)
        return 2 * c + i % 2, q + c % 2 * (zs - 1 - 2 * q)

    def dest_of(r):
        return holder(aux * rows + r)

    src_aux, src_row = row // rows, row % rows

    load_d = pltpu.make_async_copy(density_hbm.at[:, 0], staged.at[0], load_sem.at[0])
    load_p = [
        pltpu.make_async_copy(fields_hbm.at[k, :, 0], staged.at[1 + k], load_sem.at[1 + k])
        for k in range(2)
    ]
    load_t = pltpu.make_async_copy(tensor_hbm, integrals, load_sem.at[3])
    load_d.start()
    load_p[0].start()
    load_p[1].start()
    load_t.start()
    load_m = pltpu.make_async_copy(metric_hbm.at[0], metric, load_sem.at[4])
    load_m.start()

    barrier = pltpu.get_barrier_semaphore()
    greeted = 0

    def greet(a, b):
        pl.semaphore_signal(barrier, inc=1, device_id={"aux": a, "orb": b}, device_id_type=MESH)

    for step in range(1, 2 * zs):
        e = (2 * z + core + step) % (2 * zs)
        greet(2 * col + e % 2, e // 2)
    greeted += 2 * zs - 1
    for offset in (-2, -1, 1, 2):
        to_aux, to_z = holder(row + offset)

        @pl.when(to_aux // 2 != col)
        def _():
            greet(to_aux, to_z)

    place = row % (2 * zs)
    near_end = (place < 2) | (place >= 2 * zs - 2)
    at_end = (place < 1) | (place >= 2 * zs - 1)
    for step in range(1, 2 * xs):
        e = (2 * x + core + step) % (2 * xs)

        @pl.when(e // 2 != x)
        def _():
            greet(2 * xs * y + e, z)

    for step in range(1, 2 * ys):
        e = (2 * y + core + step) % (2 * ys)

        @pl.when(e // 2 != y)
        def _():
            greet(2 * (e // 2 * xs + x) + e % 2, z)

    for step in range(1, xs * ys):
        c = (col + step) % (xs * ys)

        @pl.when((c % xs != x) & (c // xs != y))
        def _():
            greet(2 * c + core, z)

    greeted += 2 * (xs - 1) + 2 * (ys - 1) + (xs - 1) * (ys - 1)

    first_row = aux * rows
    column = first_row + z - half

    def mask_of(r):
        there = (pattern[r, z] == 1) & (column + r >= 0) & (column + r < total_rows)
        return jnp.where(there, 1, 0)

    for r in range(rows):
        keep_src[r] = jnp.full((8, blk), mask_of(r), jnp.int32)

    load_d.wait()
    for r in range(rows):
        factor = jnp.full((blk, blk), mask_of(r).astype(F32), F32).astype(BF16)
        staged[0, r] = staged[0, r] * factor

    pl.semaphore_wait(barrier, greeted + jnp.where(near_end, 1, 0) + jnp.where(at_end, 1, 0))

    def send_in(mat, r):
        to_aux, to_z = dest_of(r)
        here = (to_aux == aux) & (to_z == z)
        dst = win1.at[mat, z, pl.ds(own_lo, blk)]

        @pl.when(here)
        def _():
            pltpu.make_async_copy(staged.at[mat, r], dst, in_recv.at[mat, z]).start()

        @pl.when(jnp.logical_not(here))
        def _():
            remote(staged.at[mat, r], dst, in_send.at[mat, r], in_recv.at[mat, z], to_aux, to_z).start()

    def send_keep(r):
        to_aux, to_z = dest_of(r)
        here = (to_aux == aux) & (to_z == z)

        @pl.when(here)
        def _():
            pltpu.make_async_copy(keep_src.at[r], keep.at[z], keep_recv.at[z]).start()

        @pl.when(jnp.logical_not(here))
        def _():
            remote(keep_src.at[r], keep.at[z], keep_send.at[r], keep_recv.at[z], to_aux, to_z).start()

    for r in range(rows):
        send_in(0, r)
    for r in range(rows):
        send_keep(r)
    for k in range(2):
        load_p[k].wait()
        for r in range(rows):
            factor = jnp.full((blk, blk), mask_of(r).astype(F32), F32).astype(BF16)
            staged[1 + k, r] = staged[1 + k, r] * factor
        for r in range(rows):
            send_in(1 + k, r)

    def slots_of(t):
        return max(0, t - half), min(slots, t + half)

    def message(win, phase, mat, index, t, offset):
        to = t - offset
        lo, hi = slots_of(to)
        to_aux, to_z = holder(row + offset)
        return remote(
            win.at[mat, pl.ds(lo + offset, hi - lo), pl.ds(t * blk, blk)],
            win.at[mat, pl.ds(lo, hi - lo), pl.ds(to * blk, blk)],
            win_send.at[phase, mat, index], win_recv.at[phase, mat, to], to_aux, to_z,
        )

    def got(win, phase, mat, t):
        lo, hi = slots_of(t)
        landed(win.at[mat, pl.ds(lo, hi - lo), pl.ds(t * blk, blk)], win_recv.at[phase, mat, t])

    plan = (
        (
            ((), ((half, 2), (half, -1), (half, 1))),
            ((3, 2), ((3, 2), (2, 2), (3, 1), (2, 1))),
            ((1, 0), ((1, 1),)),
            ((5, 6, 7), ()),
        ),
        (
            ((), ((half, 1), (half, -2), (half, -1))),
            ((5, 6), ((5, -2), (5, -1), (6, -1))),
            ((7,), ()),
            ((3, 2, 1, 0), ()),
        ),
    )

    def advance(win, phase, mat, step):
        for c in range(2):
            @pl.when(core == c)
            def _():
                waits, sends = plan[c][step - 1]
                index = sum(len(plan[c][j][1]) for j in range(step - 1))
                for t in waits:
                    got(win, phase, mat, t)
                for t, offset in sends:
                    message(win, phase, mat, index, t, offset).start()
                    index += 1

    def arrived(mat):
        for u in range(slots):
            landed(win1.at[mat, u, pl.ds(own_lo, blk)], in_recv.at[mat, u])
        for u in range(slots):
            lhs1[mat, :, pl.ds(u * blk, blk)] = win1[mat, u, pl.ds(own_lo, blk)]

    def kept(s, value):
        mask = jnp.broadcast_to(keep[s, pl.ds(0, 1), :], (blk, blk))
        return jnp.where(mask > 0, value, 0.0)

    def rows_of(s):
        lo, hi = max(0, s - half + 1), min(slots, s + half + 1)
        return pl.ds(lo * blk, (hi - lo) * blk)

    def square():
        def body(s, carry):
            value = jnp.dot(lhs1[0, :, rows_of(s)], win1[0, s, rows_of(s)], preferred_element_type=F32)
            win2[0, s, pl.ds(own_lo, blk)] = kept(s, value).astype(BF16)
            return carry

        for s in range(slots):
            body(s, 0)
        for s in range(slots):
            lhs2[0, :, pl.ds(s * blk, blk)] = win2[0, s, pl.ds(own_lo, blk)]

    def first(k):
        def body(s, carry):
            value = jnp.dot(lhs1[0, :, rows_of(s)], win1[1 + k, s, rows_of(s)], preferred_element_type=F32)
            value = value + jnp.dot(lhs1[1 + k, :, rows_of(s)], win1[0, s, rows_of(s)], preferred_element_type=F32)
            win2[1 + k, s, pl.ds(own_lo, blk)] = kept(s, value).astype(BF16)
            return carry

        for s in range(slots):
            body(s, 0)
        for s in range(slots):
            lhs2[1 + k, :, pl.ds(s * blk, blk)] = win2[1 + k, s, pl.ds(own_lo, blk)]

    def send_out(k, s):
        here = (src_aux == aux) & (z == s)
        dst = out.at[k, src_row, 0]

        @pl.when(here)
        def _():
            pltpu.make_async_copy(result.at[k, s], dst, out_recv.at[k, src_row]).start()

        @pl.when(jnp.logical_not(here))
        def _():
            remote(result.at[k, s], dst, out_send.at[k, s], out_recv.at[k, src_row], src_aux, s).start()

    def second(k):
        def body(s, carry):
            value = jnp.dot(lhs2[0, :, rows_of(s)], win2[1 + k, s, rows_of(s)], preferred_element_type=F32)
            value = value + jnp.dot(lhs2[1 + k, :, rows_of(s)], win2[0, s, rows_of(s)], preferred_element_type=F32)
            value = 2.0 * win2[1 + k, s, pl.ds(own_lo, blk)].astype(F32) - value
            result[k, s] = kept(s, value).astype(BF16)
            send_out(k, s)
            return carry

        for s in range(slots):
            body(s, 0)

    done = 4
    order = (
        "D1", "P1", "D2", "S1", "P2", "D3", "D4", "Q1",
        "P3", "S2", "P4", "F1", "Q2", "S3", "S4", "G1",
        "F2", "Q3", "G2", "F3", "Q4", "F4", "G3", "G4",
    )
    item_of = {"D": 0, "P": 1, "S": 2, "Q": 3, "F": 4, "G": 5}
    for word in order:
        item, step = item_of[word[0]], int(word[1])
        phase, mat = item // 3, item % 3
        if step == 1 and phase == 0:
            arrived(mat)
        if step == 1 and phase == 1:
            if mat == 0:
                for u in range(slots):
                    landed(keep.at[u], keep_recv.at[u])
                square()
            else:
                first(mat - 1)
        advance(win1 if phase == 0 else win2, phase, mat, step)
        if step == done and phase == 1 and mat > 0:
            second(mat - 1)

    fitted = fit_blocks[0]

    def over_x(d):
        return 2 * (y * xs + (x + d) % xs) + core

    def over_y(d):
        return 2 * (((y + d) % ys) * xs + x) + core

    pending = []

    def spread(src, got_there, count, ss, rs, target):
        copies = [
            remote(src, got_there.at[d - 1], ss.at[d - 1], rs.at[d - 1], target(d), z)
            for d in range(1, count)
        ]
        for c in copies:
            c.start()
        pending.extend(copies)
        return copies

    def added(src, got_there, copies):
        value = src[...]
        for d, c in enumerate(copies):
            c.wait_recv()
            value = value + got_there[d]
        return value

    def piece_of(k):
        for r in range(rows):
            landed(out.at[k, r, 0], out_recv.at[k, r])
        value = jnp.zeros((blk, blk), BF16)
        for r in range(rows):
            chosen = jnp.where(fitted == first_row + r, 1.0, 0.0)
            value = value + out[k, r, 0] * jnp.full((blk, blk), chosen, F32).astype(BF16)
        piece[k] = value

    count_aux = integrals.shape[0]

    def contract(k):
        def body(step, acc):
            rows_of = piece_f[k, pl.ds(pl.multiple_of(step * 8, 8), 8)]
            for j in range(8):
                lanes = pl.ds(pl.multiple_of(step * 8 * blk + j * blk, blk), blk)
                acc = acc + integrals[:, lanes].astype(F32) * rows_of[j : j + 1]
            return acc

        acc = lax.fori_loop(0, blk // 8, body, jnp.zeros((count_aux, blk), F32))
        wide = jnp.concatenate([acc, jnp.zeros((blk - count_aux, blk), F32)], axis=0)
        part[pl.ds(k, 1)] = jnp.sum(wide.T, axis=0, keepdims=True)

    def x_cores(d):
        return 2 * xs * y + (2 * x + core + d) % (2 * xs)

    def y_cores(d):
        e = (2 * y + core + d) % (2 * ys)
        return 2 * (e // 2 * xs + x) + e % 2

    top, low = pl.ds(0, blk // 2), pl.ds(blk // 2, blk // 2)
    piece_of(0)
    whole_1 = spread(piece.at[0], got_x.at[0], 2 * xs, fx_send.at[0], fx_recv.at[0], x_cores)
    piece_x[0] = added(piece.at[0], got_x.at[0], whole_1)
    whole_2 = spread(piece_x.at[0], got_y.at[0], ys, fy_send.at[0], fy_recv.at[0], over_y)
    piece_of(1)
    top_1 = spread(piece.at[1, top], got_x.at[1, :, top], 2 * xs, fx_send.at[1], fx_recv.at[1], x_cores)
    low_1 = spread(piece.at[1, low], got_x.at[1, :, low], 2 * ys, fx_send.at[2], fx_recv.at[2], y_cores)
    piece_f[0] = added(piece_x.at[0], got_y.at[0], whole_2).astype(F32)
    piece_x[1, top] = added(piece.at[1, top], got_x.at[1, :, top], top_1)
    top_2 = spread(piece_x.at[1, top], got_y.at[1, :, top], ys, fy_send.at[1], fy_recv.at[1], over_y)
    piece_x[1, low] = added(piece.at[1, low], got_x.at[1, :, low], low_1)
    low_2 = spread(piece_x.at[1, low], got_y.at[1, :, low], xs, fy_send.at[2], fy_recv.at[2], over_x)
    load_t.wait()
    contract(0)
    piece_f[1, top] = added(piece_x.at[1, top], got_y.at[1, :, top], top_2).astype(F32)
    piece_f[1, low] = added(piece_x.at[1, low], got_y.at[1, :, low], low_2).astype(F32)
    contract(1)

    e = 2 * z + core
    parts_z[e] = part[...]
    z_copies = []
    for d in range(1, 2 * zs):
        f = (e + d) % (2 * zs)
        z_copies.append(remote(part, parts_z.at[e], z_send.at[d - 1], z_recv.at[d - 1], 2 * col + f % 2, f // 2))
    for c in z_copies:
        c.start()
    for c in z_copies:
        c.wait_recv()
    for c in range(2):
        total = parts_z[c]
        for d in range(1, zs):
            total = total + parts_z[2 * d + c]
        sums[2 * col + c] = total
    mine = sums.at[pl.ds(2 * col, 2)]
    g_copies = [
        remote(mine, mine, g_send.at[d - 1], g_recv.at[d - 1], 2 * ((col + d) % (xs * ys)) + core, z)
        for d in range(1, xs * ys)
    ]
    for c in g_copies:
        c.start()
    for c in g_copies:
        c.wait_recv()

    load_m.wait()
    lane = lax.broadcasted_iota(jnp.int32, (1, blk), 1)
    acc = [jnp.zeros((count_aux, blk), F32) for _ in range(2)]
    for group_of in range(naux // 4):
        pieces = jnp.concatenate([sums[4 * group_of + j] for j in range(4)], axis=0)
        by96, by64, by32 = (pltpu.roll(pieces, shift, 1) for shift in (96, 64, 32))
        for k in range(2):
            one = pieces[k : k + 1]
            two = by96[2 + k : 3 + k]
            three = by64[4 + k : 5 + k]
            four = by32[6 + k : 7 + k]
            filled = (
                jnp.where(lane < 96, one, two),
                jnp.where(lane < 64, two, three),
                jnp.where(lane < 32, three, four),
            )
            for j, values in enumerate(filled):
                acc[k] = acc[k] + metric[:, pl.ds((3 * group_of + j) * blk, blk)] * values
    for k in range(2):
        wide = jnp.concatenate([acc[k], jnp.zeros((blk - count_aux, blk), F32)], axis=0)
        coefficients[0, pl.ds(k, 1)] = jnp.sum(wide.T, axis=0, keepdims=True)[:, :count_aux]

    for c in pending + z_copies + g_copies:
        c.wait_send()
    for r in range(rows):
        to_aux, to_z = dest_of(r)

        @pl.when(jnp.logical_not((to_aux == aux) & (to_z == z)))
        def _():
            for mat in range(3):
                dst = win1.at[mat, z, pl.ds(own_lo, blk)]
                remote(staged.at[mat, r], dst, in_send.at[mat, r], in_recv.at[mat, z], to_aux, to_z).wait_send()
            remote(keep_src.at[r], keep.at[z], keep_send.at[r], keep_recv.at[z], to_aux, to_z).wait_send()
    for s in range(slots):
        @pl.when(jnp.logical_not((src_aux == aux) & (z == s)))
        def _():
            for k in range(2):
                remote(
                    result.at[k, s], out.at[k, src_row, 0], out_send.at[k, s], out_recv.at[k, src_row], src_aux, s
                ).wait_send()
    for c in range(2):
        @pl.when(core == c)
        def _():
            sends = [one for stage in plan[c] for one in stage[1]]
            for phase, win in enumerate((win1, win2)):
                for mat in range(3):
                    for index, (t, offset) in enumerate(sends):
                        message(win, phase, mat, index, t, offset).wait_send()


def solution(mesh):
    naux, zs = mesh.shape["aux"], mesh.shape["orb"]
    side = {32: (4, 4), 8: (2, 2), 4: (1, 2), 2: (1, 1)}[naux]
    ys, xs = side

    def on_device(band_pattern, density_in, field_terms, fit_blocks, tensor, metric_inv):
        rows = density_in.shape[0]
        slots = zs
        blk = density_in.shape[2]
        count_aux = tensor.shape[1]
        dma = pltpu.SemaphoreType.DMA
        vmem = pltpu.VMEM
        block = (blk, blk)
        in_hbm = pl.BlockSpec(memory_space=pltpu.HBM)
        smem = pl.BlockSpec(memory_space=pltpu.SMEM)
        in_vmem = pl.BlockSpec(memory_space=pltpu.VMEM)
        return pl.pallas_call(
            functools.partial(ring_kernel, (ys, xs, zs, rows, slots)),
            out_shape=(
                jax.ShapeDtypeStruct(field_terms.shape, BF16),
                jax.ShapeDtypeStruct((1, 2, count_aux), F32),
            ),
            in_specs=[smem, smem, in_hbm, in_hbm, in_hbm, in_hbm],
            out_specs=(in_vmem, in_vmem),
            scratch_shapes=[
                vmem((naux, 2, blk), F32),
                vmem((count_aux, naux * count_aux), F32),
                vmem((3, rows, *block), BF16),
                vmem((rows, 8, blk), jnp.int32),
                vmem((slots, 8, blk), jnp.int32),
                vmem((3, slots, slots * blk, blk), BF16),
                vmem((3, slots, slots * blk, blk), BF16),
                vmem((3, blk, slots * blk), BF16),
                vmem((3, blk, slots * blk), BF16),
                vmem((2, slots, *block), BF16),
                vmem((count_aux, blk * blk), BF16),
                vmem((2, *block), BF16),
                vmem((2, *block), BF16),
                vmem((2, 2 * max(xs, ys) - 1, *block), BF16),
                vmem((2, max(xs, ys) - 1, *block), BF16),
                vmem((2, *block), F32),
                vmem((2, blk), F32),
                vmem((2 * zs, 2, blk), F32),
                dma((5,)),
                dma((3, rows)), dma((3, slots)),
                dma((rows,)), dma((slots,)),
                dma((2, 3, slots)), dma((2, 3, slots)),
                dma((2, slots)), dma((2, rows)),
                dma((3, 2 * max(xs, ys) - 1)), dma((3, 2 * max(xs, ys) - 1)),
                dma((3, max(xs, ys) - 1)), dma((3, max(xs, ys) - 1)),
                dma((2 * zs,)), dma((2 * zs,)),
                dma((xs * ys,)), dma((xs * ys,)),
            ],
            compiler_params=pltpu.CompilerParams(
                collective_id=0, has_side_effects=True, vmem_limit_bytes=53 << 20
            ),
        )(
            band_pattern, fit_blocks, density_in, field_terms,
            tensor.reshape(count_aux, blk * blk), metric_inv,
        )

    in_specs = (
        P("aux", None),
        P("aux", "orb", None, None),
        P(None, "aux", "orb", None, None),
        P(),
        P(None, "aux", "orb", None),
        P(None, "aux", None),
    )
    out_specs = (P(None, "aux", "orb", None, None), P(None, None, "aux"))
    return jax.shard_map(
        on_device, mesh=mesh, in_specs=in_specs, out_specs=out_specs, check_vma=False
    )
```
